32 devices in a mesh: groups: 2 (over x), kv: 16 (over z, y, core).
Axes of the slice: x: 2, y: 2, z: 4, core: 2. Of those that a mesh axis runs over, the one named last changes fastest.
Arguments:
- queries: bfloat16 [2, 64, 16384], P(None, ('groups', 'kv')), parts along dimension 1, may hold values from -90 to 90
- new_kv: bfloat16 [2, 2, 64, 1024], P(None, None, ('groups', 'kv')), parts along dimension 2, may hold values from -41 to 41
- root_kv: bfloat16 [128, 2, 128, 1024], P(('groups', 'kv')), parts along dimension 0, may hold values from -24 to 24
- branch_kv: bfloat16 [128, 2, 128, 1024], P(('groups', 'kv')), parts along dimension 0, may hold values from -24 to 24
- tail_kv: bfloat16 [64, 2, 512, 1024], P(('groups', 'kv')), parts along dimension 0, may hold values from -24 to 24
- parent: int32 [98], P('groups'), parts along dimension 0, may hold values from 0 to 16, as said below
- node_len: int32 [98], P('groups'), parts along dimension 0, may hold values from 1 to 8192, as said below
- leaf_of: int32 [64], P('groups'), parts along dimension 0, may hold values from 17 to 48, as said below
- branch_slot: int32 [128], P('groups'), parts along dimension 0, may hold values from 1 to 49, as said below
Outputs:
- attended: bfloat16 [2, 64, 16384], P(None, ('groups', 'kv')), parts along dimension 1
The draws below stay inside these ranges and needn't reach their ends.
There are 2 independent parts, one for each index of `groups`. The reference program is written for one: setup_inputs(seed, part) draws one part's arguments, and reference() takes and returns one part's arrays. A program takes and returns all parts, laid end to end along the dimension named above; each array names one. Nothing has to cross between parts.
Inputs may be any that keep to these rules, and one draw needn't show every extreme that they name: Node 0 is the root and its own parent; nodes 1 to 16 are branch prefixes with parent 0; nodes 17 to 48 are private tails, each with a branch prefix as parent. At most 6 tails share a branch prefix, and some branch prefix has exactly 6. node_len[0] = 8192; a branch prefix holds 1 to 512 tokens and a tail 1 to 512; some branch prefix and some tail hold exactly those most. `leaf_of`: every tail node is the leaf of exactly one request. `branch_slot`: A branch prefix of L tokens owns exactly ceil(L / 128) slots, which hold its tokens in order of slot index, 128 to a slot, the last one partly; all other slots hold 49.
All inputs are finite; a program needn't handle non-finite values.
Results may differ from the reference program's by a relative error of at most 0.002.
Values may be sent and summed in bfloat16 or wider, within the bound.
A program may use at most 192 MiB of HBM per device.

```python
import jax
import jax.numpy as jnp
from jax import lax

QH = 128
KVH = 8
HD = 128
BLOCK = 128
ROOT_DEV = 4
BR_DEV = 4
BRANCH = 16
GROUP = 16
REQ = 32
CAP = 6
ROOT_SLOTS = 64
BR_SLOTS = 64
BR_MAX_BLOCKS = 4
TAIL_LEN = 512
NODES = 49
N_KV = 16


def tree_tables(key):
    request_ids = jnp.arange(REQ, dtype=jnp.int32)
    labels = jnp.where(request_ids < CAP, 0, 1 + (request_ids - CAP) % (BRANCH - 1)).astype(jnp.int32)
    relabel = jax.random.permutation(jax.random.fold_in(key, 1), BRANCH).astype(jnp.int32)
    leaf_branch = (1 + relabel[labels]).astype(jnp.int32)
    parent_table = jnp.concatenate([jnp.zeros((1 + BRANCH,), jnp.int32), leaf_branch])
    longest = BR_MAX_BLOCKS * BLOCK
    branch_len = jax.random.randint(jax.random.fold_in(key, 2), (BRANCH,), 1, longest + 1, dtype=jnp.int32)
    branch_len = branch_len.at[relabel[1]].set(longest)
    tail_len = jax.random.randint(jax.random.fold_in(key, 3), (REQ,), 1, TAIL_LEN + 1, dtype=jnp.int32)
    tail_len = tail_len.at[0].set(TAIL_LEN)
    length_table = jnp.concatenate([jnp.full((1,), ROOT_SLOTS * BLOCK, jnp.int32), branch_len, tail_len])
    leaf_table = (BRANCH + 1 + jax.random.permutation(jax.random.fold_in(key, 4), REQ)).astype(jnp.int32)
    block_counts = (branch_len + BLOCK - 1) // BLOCK
    block_ends = jnp.cumsum(block_counts).astype(jnp.int32)
    slot_ids = jnp.arange(BR_SLOTS, dtype=jnp.int32)
    owners = 1 + jnp.sum((slot_ids[:, None] >= block_ends[None, :]).astype(jnp.int32), axis=1)
    owners = jnp.where(slot_ids < block_ends[-1], owners, NODES).astype(jnp.int32)
    placing = jax.random.permutation(jax.random.fold_in(key, 5), BR_SLOTS)
    slot_table = jnp.zeros((BR_SLOTS,), jnp.int32).at[placing].set(owners)
    return (parent_table, length_table, leaf_table, slot_table)


def draw_parent(key, part):
    return tree_tables(key)[0]


def draw_node_len(key, part):
    return tree_tables(key)[1]


def draw_leaf_of(key, part):
    return tree_tables(key)[2]


def draw_branch_slot(key, part):
    return tree_tables(key)[3]


def base_queries(key):
    shape_all = (2, REQ, QH * HD)
    return 2.5 * jnp.clip(jax.random.normal(jax.random.fold_in(key, 11), shape_all, jnp.float32), -6.0, 6.0)


def draw_queries(key, part):
    query_all = base_queries(key)
    return query_all.astype(jnp.bfloat16)


def draw_new_kv(key, part):
    query_all = base_queries(key).reshape(2, REQ, KVH, GROUP, HD)
    noise = jnp.clip(jax.random.normal(jax.random.fold_in(key, 51), (2, REQ, KVH * HD), jnp.float32), -6.0, 6.0)
    key_rows = 2.5 * jnp.mean(query_all, axis=3).reshape(2, REQ, KVH * HD) + 0.5 * noise
    value_rows = 4.0 * jnp.clip(jax.random.normal(jax.random.fold_in(key, 52), (2, REQ, KVH * HD), jnp.float32), -6.0, 6.0)
    return jnp.stack([key_rows, value_rows], axis=1).astype(jnp.bfloat16)


def cache_blocks(key, salt, count, length):
    shape_all = (count, length, KVH * HD)
    key_rows = jnp.clip(jax.random.normal(jax.random.fold_in(key, salt), shape_all, jnp.float32), -6.0, 6.0)
    value_rows = 4.0 * jnp.clip(jax.random.normal(jax.random.fold_in(key, salt + 1), shape_all, jnp.float32), -6.0, 6.0)
    return (key_rows, value_rows)


def draw_root_kv(key, part):
    key_rows, value_rows = cache_blocks(key, 21, ROOT_SLOTS, BLOCK)
    return jnp.stack([key_rows, value_rows], axis=1).astype(jnp.bfloat16)


def draw_branch_kv(key, part):
    key_rows, value_rows = cache_blocks(key, 31, BR_SLOTS, BLOCK)
    return jnp.stack([key_rows, value_rows], axis=1).astype(jnp.bfloat16)


def draw_tail_kv(key, part):
    key_rows, value_rows = cache_blocks(key, 41, REQ, TAIL_LEN)
    return jnp.stack([key_rows, value_rows], axis=1).astype(jnp.bfloat16)


def setup_inputs(seed: int = 0, part: int = 0) -> dict:
    key_list = jax.random.split(jax.random.key(seed), 10)
    part_splits = jax.random.split(jax.random.fold_in(key_list[9], part), 10)
    queries = draw_queries(jax.random.fold_in(jax.random.fold_in(key_list[9], part), 71), part)
    new_kv = draw_new_kv(jax.random.fold_in(jax.random.fold_in(key_list[9], part), 71), part)
    root_kv = draw_root_kv(jax.random.fold_in(jax.random.fold_in(key_list[9], part), 71), part)
    branch_kv = draw_branch_kv(jax.random.fold_in(jax.random.fold_in(key_list[9], part), 71), part)
    tail_kv = draw_tail_kv(jax.random.fold_in(jax.random.fold_in(key_list[9], part), 71), part)
    parent = draw_parent(jax.random.fold_in(jax.random.fold_in(key_list[9], part), 71), part)
    node_len = draw_node_len(jax.random.fold_in(jax.random.fold_in(key_list[9], part), 71), part)
    leaf_of = draw_leaf_of(jax.random.fold_in(jax.random.fold_in(key_list[9], part), 71), part)
    branch_slot = draw_branch_slot(jax.random.fold_in(jax.random.fold_in(key_list[9], part), 71), part)
    return dict(queries=queries, new_kv=new_kv, root_kv=root_kv, branch_kv=branch_kv, tail_kv=tail_kv, parent=parent, node_len=node_len, leaf_of=leaf_of, branch_slot=branch_slot)


NEG_FILL = -1.0e30


def reference(queries, new_kv, root_kv, branch_kv, tail_kv, parent, node_len, leaf_of, branch_slot):
    slot_ids = jnp.arange(BR_SLOTS, dtype=jnp.int32)
    same_node = branch_slot[:, None] == branch_slot[None, :]
    before_slot = slot_ids[None, :] < slot_ids[:, None]
    ranks = jnp.sum((same_node & before_slot).astype(jnp.int32), axis=1)
    owner_len = node_len[jnp.minimum(branch_slot, NODES - 1)]
    filled = jnp.where(branch_slot < NODES, jnp.clip(owner_len - ranks * BLOCK, 0, BLOCK), 0)
    root_span = ROOT_DEV * BLOCK
    root_keys = root_kv[:, 0].reshape(N_KV, root_span, KVH, HD).astype(jnp.float32)
    root_values = root_kv[:, 1].reshape(N_KV, root_span, KVH, HD).astype(jnp.float32)
    scale = HD ** -0.5
    part_ids = jnp.arange(N_KV, dtype=jnp.int32)

    def one_request(request):
        leaf = leaf_of[request]
        branch = parent[leaf]
        sort_key = jnp.where(branch_slot == branch, ranks, BR_SLOTS + slot_ids).astype(jnp.int32)
        ordering = jnp.argsort(sort_key, stable=True)[:BR_MAX_BLOCKS].astype(jnp.int32)
        picked = branch_kv[ordering]
        counts = jnp.where(branch_slot[ordering] == branch, filled[ordering], 0)
        branch_keys = picked[:, 0].reshape(BR_MAX_BLOCKS * BLOCK, KVH, HD).astype(jnp.float32)
        branch_values = picked[:, 1].reshape(BR_MAX_BLOCKS * BLOCK, KVH, HD).astype(jnp.float32)
        branch_live = (jnp.arange(BLOCK, dtype=jnp.int32)[None, :] < counts[:, None]).reshape(-1)
        token_part = jnp.repeat((ordering // BR_DEV).astype(jnp.int32), BLOCK)
        onehot = (token_part[:, None] == part_ids[None, :]) & branch_live[:, None]
        onehot_float = onehot.astype(jnp.float32)
        tail_keys = tail_kv[request, 0].reshape(TAIL_LEN, KVH, HD).astype(jnp.float32)
        tail_values = tail_kv[request, 1].reshape(TAIL_LEN, KVH, HD).astype(jnp.float32)
        tail_live = jnp.arange(TAIL_LEN, dtype=jnp.int32) < node_len[leaf]
        fresh_keys = new_kv[:, 0, request].reshape(2, KVH, HD).astype(jnp.float32)
        fresh_values = new_kv[:, 1, request].reshape(2, KVH, HD).astype(jnp.float32)
        own_keys = jnp.concatenate([tail_keys, fresh_keys], axis=0)
        own_values = jnp.concatenate([tail_values, fresh_values], axis=0)
        results = []
        for step_index in range(2):
            query_rows = queries[step_index, request].reshape(KVH, GROUP, HD).astype(jnp.float32)
            root_scores = jnp.einsum("kgd,ntkd->kgnt", query_rows, root_keys, precision=lax.Precision.HIGHEST) * scale
            branch_scores = jnp.einsum("kgd,tkd->kgt", query_rows, branch_keys, precision=lax.Precision.HIGHEST) * scale
            branch_scores = jnp.where(branch_live[None, None, :], branch_scores, NEG_FILL)
            root_peak = jnp.max(root_scores, axis=-1)
            branch_peak = jnp.max(jnp.where(onehot[None, None], branch_scores[..., None], NEG_FILL), axis=2)
            part_peak = jnp.maximum(root_peak, branch_peak)
            root_weights = jnp.exp(root_scores - part_peak[..., None])
            token_peak = part_peak[:, :, jnp.minimum(token_part, N_KV - 1)]
            branch_weights = jnp.where(branch_live[None, None, :], jnp.exp(branch_scores - token_peak), 0.0)
            part_totals = jnp.sum(root_weights, axis=-1) + jnp.einsum("kgt,tn->kgn", branch_weights, onehot_float, precision=lax.Precision.HIGHEST)
            root_rounded = lax.optimization_barrier(root_weights.astype(jnp.bfloat16)).astype(jnp.float32)
            branch_rounded = lax.optimization_barrier(branch_weights.astype(jnp.bfloat16)).astype(jnp.float32)
            part_out = jnp.einsum("kgnt,ntkd->kgnd", root_rounded, root_values, precision=lax.Precision.HIGHEST)
            spread = branch_rounded[..., None] * onehot_float[None, None]
            part_out = part_out + jnp.einsum("kgtn,tkd->kgnd", spread, branch_values, precision=lax.Precision.HIGHEST)
            normed = part_out / part_totals[..., None]
            normed = lax.optimization_barrier(normed.astype(jnp.bfloat16)).astype(jnp.float32)
            own_live = jnp.concatenate([tail_live, jnp.arange(2, dtype=jnp.int32) <= step_index])
            own_scores = jnp.einsum("kgd,tkd->kgt", query_rows, own_keys, precision=lax.Precision.HIGHEST) * scale
            own_scores = jnp.where(own_live[None, None, :], own_scores, NEG_FILL)
            own_peak = jnp.max(own_scores, axis=-1)
            own_weights = jnp.where(own_live[None, None, :], jnp.exp(own_scores - own_peak[..., None]), 0.0)
            own_total = jnp.sum(own_weights, axis=-1)
            own_rounded = lax.optimization_barrier(own_weights.astype(jnp.bfloat16)).astype(jnp.float32)
            own_out = jnp.einsum("kgt,tkd->kgd", own_rounded, own_values, precision=lax.Precision.HIGHEST)
            top = jnp.maximum(jnp.max(part_peak, axis=-1), own_peak)
            part_factor = part_totals * jnp.exp(part_peak - top[..., None])
            own_factor = jnp.exp(own_peak - top)
            numer = jnp.sum(part_factor[..., None] * normed, axis=2) + own_factor[..., None] * own_out
            denom = jnp.sum(part_factor, axis=-1) + own_factor * own_total
            outputs = numer / denom[..., None]
            results.append(outputs.reshape(QH * HD).astype(jnp.bfloat16))
        return jnp.stack(results)

    gathered = lax.map(one_request, jnp.arange(REQ, dtype=jnp.int32))
    return jnp.swapaxes(gathered, 0, 1)
```

```python
import functools

import jax
import jax.numpy as jnp
from jax import lax
from jax.experimental import pallas as pl
from jax.experimental.pallas import tpu as pltpu
from jax.sharding import PartitionSpec as P

QH = 128
KVH = 8
HD = 128
GROUP = QH // KVH
HEADS = KVH // 2
PAIR = 2
MASKED = -1e30
UNIT = HD**-0.5 * 1.4426950408889634
LANES = 256
EXTRA = 16
LAG_OTHER = 1
LAG_MERGE = 2
LAG_LAST = 3


def matmul(a, b, dims):
    return lax.dot_general(a, b, (dims, ((), ())), preferred_element_type=jnp.float32)


def attend(scores):
    top = functools.reduce(jnp.maximum, [jnp.max(s, axis=0, keepdims=True) for s in scores]) * UNIT
    weights = [jnp.exp2(s * UNIT - top) for s in scores]
    return top, weights


def kernel(
    devices, steps, req_here,
    parent, node_len, leaf_of, branch_slot,
    q_in, new_ref, root_hbm, branch_hbm, tail_hbm,
    out_ref,
    qsrc, qown, qfar, root, branch, tail, vt, kaug, qaug, tl_ref, fresh,
    own_o, own_s, put_o, put_s, got_o, got_s, fold_o, fold_s, all_o, all_s, tacc, tst,
    hbm_sem, kv_s, kv_r, gz_s, gz_r, gy_s, gy_r, y_s, y_r, z_s, z_r,
):
    depth = devices // 4
    rows = steps * req_here * GROUP
    plane = depth * 2 * rows
    half_dim = HD // 2
    me = lax.axis_index("kv")
    core = lax.rem(me, 2)
    yy = lax.rem(me // 2, 2)
    zz = me // 4
    core_peer = me + 1 - 2 * core
    y_peer = me + 2 - 4 * yy
    n_root = root.shape[1]
    n_branch = branch.shape[1]
    block_len = root.shape[3]
    blocks = 2 * (n_root + n_branch)
    half_cols = HEADS * HD

    def device(z, k):
        return z * 4 + yy * 2 + k

    def remote(src, dst, send, recv, peer):
        return pltpu.make_async_remote_copy(
            src_ref=src, dst_ref=dst, send_sem=send, recv_sem=recv,
            device_id={"kv": peer}, device_id_type=pl.DeviceIdType.MESH,
        )

    def half(ref, k):
        return ref.at[:, :, :, pl.ds(pl.multiple_of(k * half_cols, half_cols), half_cols)]

    loads = [
        pltpu.make_async_copy(half(root_hbm, core), root.at[core], hbm_sem.at[0]),
        pltpu.make_async_copy(half(branch_hbm, core), branch.at[core], hbm_sem.at[1]),
        pltpu.make_async_copy(tail_hbm, tail, hbm_sem.at[2]),
    ]
    shares = [
        remote(half(root_hbm, 1 - core), root.at[core], kv_s.at[0], kv_r.at[0], core_peer),
        remote(half(branch_hbm, 1 - core), branch.at[core], kv_s.at[1], kv_r.at[1], core_peer),
    ]
    shares_in = [
        remote(root.at[core], root.at[1 - core], kv_s.at[0], kv_r.at[0], core_peer),
        remote(branch.at[core], branch.at[1 - core], kv_s.at[1], kv_r.at[1], core_peer),
    ]
    for load in loads:
        load.start()

    barrier = pltpu.get_barrier_semaphore()
    peers = [core_peer, y_peer]
    for o in range(1, depth):
        z = lax.rem(zz + o, depth)
        peers += [device(z, core), device(z, 1 - core)]
    for peer in peers:
        pl.semaphore_signal(
            barrier, inc=1, device_id={"kv": peer}, device_id_type=pl.DeviceIdType.MESH
        )

    def lay_out(h):
        pieces = []
        for s in range(steps):
            for g in range(GROUP):
                cols = pl.ds(pl.multiple_of((h * GROUP + g) * HD, HD), HD)
                pieces.append(q_in[s, :, cols].astype(jnp.float32))
        qsrc[h] = jnp.concatenate(pieces, axis=0).astype(jnp.bfloat16)

    @pl.loop(0, KVH)
    def _(h):
        lay_out(h)

    pl.semaphore_wait(barrier, len(peers))

    @pl.loop(0, HEADS)
    def _(c):
        for k in (core, 1 - core):
            src = qsrc.at[k * HEADS + c]
            dst = qown.at[c, zz * 2 + core]
            for o in range(depth - 1, 0, -1):
                z = lax.rem(zz + o, depth)
                remote(
                    src, dst, gz_s.at[c, z * 2 + k], gz_r.at[c, zz * 2 + core], device(z, k)
                ).start()
        remote(
            qsrc.at[(1 - core) * HEADS + c], qown.at[c, zz * 2 + core],
            gz_s.at[c, zz * 2 + 1 - core], gz_r.at[c, zz * 2 + core], core_peer,
        ).start()
        qown[c, zz * 2 + core] = qsrc[core * HEADS + c]

    for share in shares:
        share.start()

    def gather_z_in(c):
        copies = []
        for o in range(depth):
            for k in (core, 1 - core)[o == 0 :]:
                i = lax.rem(zz + o, depth) * 2 + k
                part = qown.at[c, i]
                copies.append(remote(part, part, gz_s.at[c, i], gz_r.at[c, i], y_peer))
        return copies

    def gather_y(c):
        return remote(qown.at[c], qfar.at[c], gy_s.at[c], gy_r.at[c], y_peer)

    def send_y(c):
        return (
            remote(put_o.at[c], got_o.at[c], y_s.at[c, 0], y_r.at[c, 0], y_peer),
            remote(put_s.at[c], got_s.at[c], y_s.at[c, 1], y_r.at[c, 1], y_peer),
        )

    def send_z(c, z, k):
        h = core * HEADS + c
        return (
            remote(
                fold_o.at[c, z * 2 + k], all_o.at[h, zz], z_s.at[c, z * 2 + k, 0], z_r.at[h, zz, 0], device(z, k)
            ),
            remote(
                fold_s.at[c, z * 2 + k], all_s.at[h, zz], z_s.at[c, z * 2 + k, 1], z_r.at[h, zz, 1], device(z, k)
            ),
        )

    def send_z_in(c, k, first):
        h = k * HEADS + c
        copies = []
        for o in range(first, depth):
            z = lax.rem(zz + o, depth)
            copies += [
                remote(all_o.at[h, z], all_o.at[h, z], z_s.at[0, 0, 0], z_r.at[h, z, 0], y_peer),
                remote(all_s.at[h, z], all_s.at[h, z], z_s.at[0, 0, 1], z_r.at[h, z, 1], y_peer),
            ]
        return copies

    def tables():
        slots = 2 * n_branch
        first_slot = (me // 2) * slots
        slot_nodes = [branch_slot[first_slot + j] for j in range(slots)]

        def count_rank(i, ranks):
            node = branch_slot[i]
            return tuple(
                rank + jnp.where((node == slot_nodes[j]) & (i < first_slot + j), 1, 0)
                for j, rank in enumerate(ranks)
            )

        ranks = lax.fori_loop(0, branch_slot.shape[0], count_rank, (jnp.int32(0),) * slots)
        token = lax.broadcasted_iota(jnp.int32, (block_len, HD), 0)
        lane = lax.broadcasted_iota(jnp.int32, (block_len, HD), 1)
        for j in range(slots):
            owned = node_len[jnp.minimum(slot_nodes[j], node_len.shape[0] - 1)]
            fill = jnp.clip(owned - ranks[j] * block_len, 0, block_len)
            fill = jnp.where(slot_nodes[j] < node_len.shape[0], fill, 0)
            x = jnp.where(lane == j, 1.0, 0.0)
            x = jnp.where((lane == slots) & (token >= fill), MASKED, x)
            kaug[j] = x.astype(jnp.bfloat16)
        tile = 16
        lane = lax.broadcasted_iota(jnp.int32, (tile, HD), 1)
        which = lax.rem(lax.broadcasted_iota(jnp.int32, (tile, HD), 0), req_here)
        slot_of_lane = jnp.full((tile, HD), -1, jnp.int32)
        for j in range(slots):
            slot_of_lane = jnp.where(lane == j, slot_nodes[j], slot_of_lane)
        for y in range(2):
            for i in range(2 * depth):
                owner = (i // 2) * 4 + y * 2 + i % 2
                node = jnp.zeros((tile, HD), jnp.int32)
                for r in range(req_here):
                    node = jnp.where(which == r, parent[leaf_of[owner * req_here + r]], node)
                x = jnp.where(node == slot_of_lane, 0.0, MASKED)
                x = jnp.where(lane < slots, x, jnp.where(lane == slots, 1.0, 0.0))
                qaug[y, i] = jnp.concatenate([x] * (rows // tile), axis=0).astype(jnp.bfloat16)
        lane = lax.broadcasted_iota(jnp.int32, (1, PAIR * rows), 1)
        for r in range(req_here):
            tl_ref[r : r + 1, :] = jnp.where(
                lax.rem(lane, req_here) == r, node_len[leaf_of[me * req_here + r]], 0
            )
        fresh[...] = jnp.zeros_like(fresh)
        for s in range(steps):
            for kv in range(2):
                fresh[kv, s * req_here : (s + 1) * req_here, :] = new_ref[s, kv]
        vt[:, HD:, :] = jnp.ones((HEADS, EXTRA, vt.shape[2]), jnp.bfloat16)

    def head_cols(k):
        return pl.ds(pl.multiple_of(k * HD, HD), HD)

    def fold(x, part):
        return jnp.concatenate([x[:half_dim, part], x[half_dim:, part]], axis=1)

    def tail_part(p):
        query = [qsrc[p * PAIR + h] for h in range(PAIR)]
        cols = [head_cols(p * PAIR + h) for h in range(PAIR)]
        scores = []
        for r in range(req_here):
            s = jnp.concatenate(
                [matmul(tail[r, 0, :, cols[h]], query[h], ((1,), (1,))) for h in range(PAIR)], axis=1
            )
            token = lax.broadcasted_iota(jnp.int32, s.shape, 0)
            scores.append(jnp.where(token < tl_ref[r : r + 1, :], s, MASKED))
        s = jnp.concatenate(
            [matmul(fresh[0, :, cols[h]], query[h], ((1,), (1,))) for h in range(PAIR)], axis=1
        )
        token = lax.broadcasted_iota(jnp.int32, s.shape, 0)
        lane = lax.broadcasted_iota(jnp.int32, s.shape, 1)
        lane_step = lax.rem(lane // (GROUP * req_here), steps)
        live = (token < steps * req_here) & (lax.rem(token, req_here) == lax.rem(lane, req_here))
        live = live & (token // req_here <= lane_step)
        scores.append(jnp.where(live, s, MASKED))
        top, weights = attend(scores)
        total = functools.reduce(jnp.add, [jnp.sum(w, axis=0, keepdims=True) for w in weights])
        weights = [w.astype(jnp.bfloat16) for w in weights]
        stat = jnp.concatenate([top, total], axis=0)
        for h in range(PAIR):
            values = [tail[r, 1, :, cols[h]] for r in range(req_here)] + [fresh[1, :, cols[h]]]
            part = slice(h * rows, (h + 1) * rows)
            out = functools.reduce(
                jnp.add, [matmul(v, w[:, part], ((0,), (0,))) for v, w in zip(values, weights)]
            )
            tacc[p * PAIR + h] = jnp.concatenate([out[:half_dim], out[half_dim:]], axis=1)
            tst[p * PAIR + h] = jnp.concatenate([stat[:, part]] * 2, axis=1)

    def turn_values(c):
        cols = head_cols(c)
        for k in range(2):
            for b in range(n_root):
                i = k * n_root + b
                vt[c, :HD, i * block_len : (i + 1) * block_len] = root[k, b, 1, :, cols].T
            for b in range(n_branch):
                i = 2 * n_root + k * n_branch + b
                vt[c, :HD, i * block_len : (i + 1) * block_len] = branch[k, b, 1, :, cols].T

    def cache_part(c, qbuf, y, keep):
        cols = head_cols(c)
        per = LANES // rows
        for i in range(plane // LANES):
            query = jnp.concatenate([qbuf[c, i * per + j] for j in range(per)], axis=0)
            mark = jnp.concatenate([qaug[y, i * per + j] for j in range(per)], axis=0)
            wide = jnp.concatenate([query, mark], axis=1)
            scores = []
            for k in range(2):
                for b in range(n_root):
                    scores.append(matmul(root[k, b, 0, :, cols], query, ((1,), (1,))))
            for k in range(2):
                for b in range(n_branch):
                    key = jnp.concatenate([branch[k, b, 0, :, cols], kaug[k * n_branch + b]], axis=1)
                    scores.append(matmul(key, wide, ((1,), (1,))))
            top, weights = attend(scores)
            weights = jnp.concatenate([w.astype(jnp.bfloat16) for w in weights], axis=0)
            out = matmul(vt[c], weights, ((1,), (0,)))
            keep(i, top, out[HD : HD + 1], out[:HD])

    def keep_own(c):
        def keep(i, top, total, out):
            own_o[c, i] = out
            own_s[c, i] = jnp.concatenate([top, total], axis=0)

        return keep

    def keep_put(c):
        def keep(i, top, total, out):
            put_o[c, i] = out.astype(jnp.bfloat16)
            put_s[c, i] = jnp.concatenate([top, total], axis=0)

        return keep

    def merge(c):
        per = LANES // rows
        for j in range(plane // LANES):
            stat_a, stat_b = own_s[c, j], got_s[c, j]
            top = jnp.maximum(stat_a[0:1], stat_b[0:1])
            wa = jnp.exp2(stat_a[0:1] - top)
            wb = jnp.exp2(stat_b[0:1] - top)
            stat = jnp.concatenate([top, stat_a[1:2] * wa + stat_b[1:2] * wb], axis=0)
            out = own_o[c, j] * wa + got_o[c, j].astype(jnp.float32) * wb
            for i in range(per):
                part = slice(i * rows, (i + 1) * rows)
                fold_o[c, j * per + i] = fold(out, part).astype(jnp.bfloat16)
                fold_s[c, j * per + i] = jnp.concatenate([stat[:, part]] * 2, axis=1)

    def finish(h):
        stats = [all_s[h, z] for z in range(depth)]
        own = tst[h]
        top = functools.reduce(jnp.maximum, [s[0:1] for s in stats] + [own[0:1]])
        scale = jnp.exp2(own[0:1] - top)
        number = tacc[h] * scale
        total = own[1:2] * scale
        for z in range(depth):
            factor = jnp.exp2(stats[z][0:1] - top)
            number = number + all_o[h, z].astype(jnp.float32) * factor
            total = total + stats[z][1:2] * factor
        out = number / total
        out = jnp.concatenate([out[:, :rows], out[:, rows:]], axis=0).T
        for s in range(steps):
            for g in range(GROUP):
                first = (s * GROUP + g) * req_here
                cols = pl.ds(pl.multiple_of((h * GROUP + g) * HD, HD), HD)
                out_ref[s, :, cols] = out[first : first + req_here].astype(jnp.bfloat16)

    tables()
    loads[2].wait()

    @pl.loop(0, KVH // PAIR // 2)
    def _(p):
        tail_part(p)

    for load in loads[:2]:
        load.wait()
    for share in shares_in:
        share.wait_recv()

    @pl.loop(0, HEADS + LAG_LAST)
    def _(t):
        @pl.when(t < HEADS)
        def _():
            for copy in gather_z_in(t):
                copy.wait_recv()
            gather_y(t).start()
            turn_values(t)
            cache_part(t, qown, yy, keep_own(t))

        @pl.when((t >= LAG_OTHER) & (t < HEADS + LAG_OTHER))
        def _():
            c = t - LAG_OTHER
            gather_y(c).wait_recv()
            cache_part(c, qfar, 1 - yy, keep_put(c))
            for copy in send_y(c):
                copy.start()

        @pl.when((t >= LAG_MERGE) & (t < HEADS + LAG_MERGE))
        def _():
            c = t - LAG_MERGE
            for copy in send_y(c):
                copy.wait_recv()
            merge(c)
            for o in range(1, depth):
                z = lax.rem(zz + o, depth)
                for copy in send_z(c, z, core) + send_z(c, z, 1 - core):
                    copy.start()
            for copy in send_z(c, zz, 1 - core):
                copy.start()
            all_o[core * HEADS + c, zz] = fold_o[c, zz * 2 + core]
            all_s[core * HEADS + c, zz] = fold_s[c, zz * 2 + core]

        @pl.when(t == HEADS - 1)
        def _():
            @pl.loop(KVH // PAIR // 2, KVH // PAIR)
            def _(p):
                tail_part(p)

        @pl.when(t >= LAG_LAST)
        def _():
            c = t - LAG_LAST
            for k, first in ((core, 1), (1 - core, 0)):
                for copy in send_z_in(c, k, first):
                    copy.wait_recv()
                finish(k * HEADS + c)

    @pl.loop(0, HEADS)
    def _(c):
        gather_y(c).wait_send()
        copies = list(send_y(c)) + gather_z_in(c)
        for o in range(depth):
            for k in (core, 1 - core)[o == 0 :]:
                copies += send_z(c, lax.rem(zz + o, depth), k)
        for copy in copies:
            copy.wait_send()

    for share in shares:
        share.wait_send()


def body(queries, new_kv, root_kv, branch_kv, tail_kv, parent, node_len, leaf_of, branch_slot):
    devices = lax.axis_size("kv")
    steps, req_here, _ = queries.shape
    rows = steps * req_here * GROUP
    depth = devices // 4
    plane = depth * 2 * rows
    n_root, _, block_len, _ = root_kv.shape
    n_branch = branch_kv.shape[0]
    tokens = 2 * (n_root + n_branch) * block_len
    bf, f32 = jnp.bfloat16, jnp.float32
    vmem = pl.BlockSpec(memory_space=pltpu.VMEM)
    smem = pl.BlockSpec(memory_space=pltpu.SMEM)
    hbm = pl.BlockSpec(memory_space=pl.ANY)
    dma = pltpu.SemaphoreType.DMA
    return pl.pallas_call(
        functools.partial(kernel, devices, steps, req_here),
        out_shape=jax.ShapeDtypeStruct(queries.shape, bf),
        in_specs=[smem] * 4 + [vmem] * 2 + [hbm] * 3,
        out_specs=vmem,
        scratch_shapes=[
            pltpu.VMEM((KVH, rows, HD), bf),
            pltpu.VMEM((HEADS, depth * 2, rows, HD), bf),
            pltpu.VMEM((HEADS, depth * 2, rows, HD), bf),
            pltpu.VMEM((2, n_root, 2, block_len, HEADS * HD), bf),
            pltpu.VMEM((2, n_branch, 2, block_len, HEADS * HD), bf),
            pltpu.VMEM(tail_kv.shape, bf),
            pltpu.VMEM((HEADS, HD + EXTRA, tokens), bf),
            pltpu.VMEM((2 * n_branch, block_len, HD), bf),
            pltpu.VMEM((2, depth * 2, rows, HD), bf),
            pltpu.VMEM((req_here, PAIR * rows), jnp.int32),
            pltpu.VMEM((2, 16, KVH * HD), bf),
            pltpu.VMEM((HEADS, plane // LANES, HD, LANES), f32),
            pltpu.VMEM((HEADS, plane // LANES, 2, LANES), f32),
            pltpu.VMEM((HEADS, plane // LANES, HD, LANES), bf),
            pltpu.VMEM((HEADS, plane // LANES, 2, LANES), f32),
            pltpu.VMEM((HEADS, plane // LANES, HD, LANES), bf),
            pltpu.VMEM((HEADS, plane // LANES, 2, LANES), f32),
            pltpu.VMEM((HEADS, depth * 2, HD // 2, 2 * rows), bf),
            pltpu.VMEM((HEADS, depth * 2, 2, 2 * rows), f32),
            pltpu.VMEM((KVH, depth, HD // 2, 2 * rows), bf),
            pltpu.VMEM((KVH, depth, 2, 2 * rows), f32),
            pltpu.VMEM((KVH, HD // 2, 2 * rows), f32),
            pltpu.VMEM((KVH, 2, 2 * rows), f32),
            dma((3,)), dma((2,)), dma((2,)),
            dma((HEADS, 2 * depth)), dma((HEADS, 2 * depth)), dma((HEADS,)), dma((HEADS,)),
            dma((HEADS, 2)), dma((HEADS, 2)), dma((HEADS, 2 * depth, 2)), dma((KVH, depth, 2)),
        ],
        compiler_params=pltpu.CompilerParams(
            collective_id=0, has_side_effects=True, vmem_limit_bytes=56 * 1024 * 1024
        ),
    )(parent, node_len, leaf_of, branch_slot, queries, new_kv, root_kv, branch_kv, tail_kv)


def solution(mesh):
    return jax.shard_map(
        body,
        mesh=mesh,
        in_specs=(
            P(None, ("groups", "kv"), None),
            P(None, None, ("groups", "kv"), None),
            P(("groups", "kv"), None, None, None),
            P(("groups", "kv"), None, None, None),
            P(("groups", "kv"), None, None, None),
            P("groups"),
            P("groups"),
            P("groups"),
            P("groups"),
        ),
        out_specs=P(None, ("groups", "kv"), None),
        check_vma=False,
    )
```

```python
import functools

import jax
import jax.numpy as jnp
from jax import lax
from jax.experimental import pallas as pl
from jax.experimental.pallas import tpu as pltpu
from jax.sharding import PartitionSpec as P

QH = 128
KVH = 8
HD = 128
GROUP = QH // KVH
HEADS = KVH // 2
PAIR = 2
MASKED = -1e30
UNIT = HD**-0.5 * 1.4426950408889634
EXTRA = 16
AHEAD = 2
LAG_WORK = 2
LAG_MERGE = 4
LAG_LAST = 6


def matmul(a, b, dims):
    return lax.dot_general(a, b, (dims, ((), ())), preferred_element_type=jnp.float32)


def attend(scores):
    top = functools.reduce(jnp.maximum, [jnp.max(s, axis=0, keepdims=True) for s in scores]) * UNIT
    weights = [jnp.exp2(s * UNIT - top) for s in scores]
    return top, weights


def kernel(
    devices, steps, req_here,
    parent, node_len, leaf_of, branch_slot,
    q_in, new_ref, root_hbm, branch_hbm, tail_hbm,
    out_ref,
    qsrc, qown, qfar, root, branch, tail, vt, kaug, qaug, tl_ref, fresh,
    own_o, own_s, put_o, put_s, got_o, got_s, fold_o, fold_s, all_o, all_s, tacc, tst,
    hbm_sem, kv_s, kv_r, gz_s, gz_r, gy_s, gy_r, y_s, y_r, z_s, z_r,
):
    depth = devices // 4
    rows = steps * req_here * GROUP
    chunks = 2 * HEADS
    lanes = depth * rows
    half_dim = HD // 2
    me = lax.axis_index("kv")
    core = lax.rem(me, 2)
    yy = lax.rem(me // 2, 2)
    zz = me // 4
    core_peer = me + 1 - 2 * core
    y_peer = me + 2 - 4 * yy
    n_root = root.shape[1]
    n_branch = branch.shape[1]
    block_len = root.shape[3]
    blocks = 2 * (n_root + n_branch)
    half_cols = HEADS * HD

    def device(z, k):
        return z * 4 + yy * 2 + k

    def remote(src, dst, send, recv, peer):
        return pltpu.make_async_remote_copy(
            src_ref=src, dst_ref=dst, send_sem=send, recv_sem=recv,
            device_id={"kv": peer}, device_id_type=pl.DeviceIdType.MESH,
        )

    def half(ref, k):
        return ref.at[:, :, :, pl.ds(pl.multiple_of(k * half_cols, half_cols), half_cols)]

    loads = [
        pltpu.make_async_copy(half(root_hbm, core), root.at[core], hbm_sem.at[0]),
        pltpu.make_async_copy(half(branch_hbm, core), branch.at[core], hbm_sem.at[1]),
        pltpu.make_async_copy(tail_hbm, tail, hbm_sem.at[2]),
    ]
    shares = [
        remote(half(root_hbm, 1 - core), root.at[core], kv_s.at[0], kv_r.at[0], core_peer),
        remote(half(branch_hbm, 1 - core), branch.at[core], kv_s.at[1], kv_r.at[1], core_peer),
    ]
    shares_in = [
        remote(root.at[core], root.at[1 - core], kv_s.at[0], kv_r.at[0], core_peer),
        remote(branch.at[core], branch.at[1 - core], kv_s.at[1], kv_r.at[1], core_peer),
    ]
    for load in loads:
        load.start()

    barrier = pltpu.get_barrier_semaphore()
    peers = [core_peer, y_peer]
    for o in range(1, depth):
        z = lax.rem(zz + o, depth)
        peers += [device(z, core), device(z, 1 - core)]
    for peer in peers:
        pl.semaphore_signal(
            barrier, inc=1, device_id={"kv": peer}, device_id_type=pl.DeviceIdType.MESH
        )

    def lay_out(h):
        pieces = []
        for s in range(steps):
            for g in range(GROUP):
                cols = pl.ds(pl.multiple_of((h * GROUP + g) * HD, HD), HD)
                pieces.append(q_in[s, :, cols].astype(jnp.float32))
        qsrc[h] = jnp.concatenate(pieces, axis=0).astype(jnp.bfloat16)

    @pl.loop(0, KVH)
    def _(h):
        lay_out(h)

    pl.semaphore_wait(barrier, len(peers))

    def gather_z_start(c):
        dst = qown.at[c * 2 + core, zz]
        for k in (core, 1 - core):
            for o in range(depth - 1, 0, -1):
                z = lax.rem(zz + o, depth)
                gather_z(c, k, dst, device(z, k)).start()
        gather_z(c, 1 - core, dst, core_peer).start()
        qown[c * 2 + core, zz] = qsrc[core * HEADS + c]

    def gather_z(c, k, dst, peer):
        return remote(
            qsrc.at[k * HEADS + c], dst, gz_s.at[c, lax.rem(k + core, 2)],
            gz_r.at[c * 2 + core, zz], peer,
        )

    for c in range(AHEAD):
        gather_z_start(c)
    for share in shares:
        share.start()

    def gather_z_in(n, z):
        return remote(qown.at[n, z], qown.at[n, z], gz_s.at[0, 0], gz_r.at[n, z], y_peer)

    def gather_z_wait(n):
        for o in range(1, depth):
            gather_z_in(n, lax.rem(zz + o, depth)).wait_recv()

        @pl.when(lax.rem(n, 2) != core)
        def _():
            gather_z_in(n, zz).wait_recv()

    def gather_z_sent(c, other):
        part = qown.at[0, pl.ds(0, depth - 1 + other)]
        return remote(part, part, gz_s.at[c, other], gz_r.at[0, 0], y_peer)

    def gather_y(n):
        return remote(qown.at[n], qfar.at[n], gy_s.at[n], gy_r.at[n], y_peer)

    def send_y(n):
        return (
            remote(put_o.at[n], got_o.at[n], y_s.at[n, 0], y_r.at[n, 0], y_peer),
            remote(put_s.at[n], got_s.at[n], y_s.at[n, 1], y_r.at[n, 1], y_peer),
        )

    def send_z(n, z):
        c = n // 2
        h = core * HEADS + c
        peer = device(z, lax.rem(n, 2))
        return (
            remote(fold_o.at[n, z], all_o.at[h, zz], z_s.at[n, 0], z_r.at[h, zz, 0], peer),
            remote(fold_s.at[n, z], all_s.at[h, zz], z_s.at[n, 1], z_r.at[h, zz, 1], peer),
        )

    def send_z_in(h, z):
        return (
            remote(all_o.at[h, z], all_o.at[h, z], z_s.at[0, 0], z_r.at[h, z, 0], y_peer),
            remote(all_s.at[h, z], all_s.at[h, z], z_s.at[0, 1], z_r.at[h, z, 1], y_peer),
        )

    def send_z_sent(n, count):
        part = pl.ds(0, count)
        return (
            remote(fold_o.at[n, part], fold_o.at[n, part], z_s.at[n, 0], z_r.at[0, 0, 0], y_peer),
            remote(fold_s.at[n, part], fold_s.at[n, part], z_s.at[n, 1], z_r.at[0, 0, 1], y_peer),
        )

    def tables():
        slots = 2 * n_branch
        first_slot = (me // 2) * slots
        slot_nodes = [branch_slot[first_slot + j] for j in range(slots)]

        def count_rank(i, ranks):
            node = branch_slot[i]
            return tuple(
                rank + jnp.where((node == slot_nodes[j]) & (i < first_slot + j), 1, 0)
                for j, rank in enumerate(ranks)
            )

        ranks = lax.fori_loop(0, branch_slot.shape[0], count_rank, (jnp.int32(0),) * slots)
        token = lax.broadcasted_iota(jnp.int32, (block_len, HD), 0)
        lane = lax.broadcasted_iota(jnp.int32, (block_len, HD), 1)
        for j in range(slots):
            owned = node_len[jnp.minimum(slot_nodes[j], node_len.shape[0] - 1)]
            fill = jnp.clip(owned - ranks[j] * block_len, 0, block_len)
            fill = jnp.where(slot_nodes[j] < node_len.shape[0], fill, 0)
            x = jnp.where(lane == j, 1.0, 0.0)
            x = jnp.where((lane == slots) & (token >= fill), MASKED, x)
            kaug[j] = x.astype(jnp.bfloat16)
        tile = 16
        lane = lax.broadcasted_iota(jnp.int32, (tile, HD), 1)
        which = lax.rem(lax.broadcasted_iota(jnp.int32, (tile, HD), 0), req_here)
        slot_of_lane = jnp.full((tile, HD), -1, jnp.int32)
        for j in range(slots):
            slot_of_lane = jnp.where(lane == j, slot_nodes[j], slot_of_lane)
        for y in range(2):
            for i in range(2 * depth):
                owner = (i % depth) * 4 + y * 2 + i // depth
                node = jnp.zeros((tile, HD), jnp.int32)
                for r in range(req_here):
                    node = jnp.where(which == r, parent[leaf_of[owner * req_here + r]], node)
                x = jnp.where(node == slot_of_lane, 0.0, MASKED)
                x = jnp.where(lane < slots, x, jnp.where(lane == slots, 1.0, 0.0))
                qaug[y, i] = jnp.concatenate([x] * (rows // tile), axis=0).astype(jnp.bfloat16)
        lane = lax.broadcasted_iota(jnp.int32, (1, PAIR * rows), 1)
        for r in range(req_here):
            tl_ref[r : r + 1, :] = jnp.where(
                lax.rem(lane, req_here) == r, node_len[leaf_of[me * req_here + r]], 0
            )
        fresh[...] = jnp.zeros_like(fresh)
        for s in range(steps):
            for kv in range(2):
                fresh[kv, s * req_here : (s + 1) * req_here, :] = new_ref[s, kv]
        vt[:, HD:, :] = jnp.ones((HEADS, EXTRA, vt.shape[2]), jnp.bfloat16)

    def head_cols(k):
        return pl.ds(pl.multiple_of(k * HD, HD), HD)

    def fold(x, part):
        return jnp.concatenate([x[:half_dim, part], x[half_dim:, part]], axis=1)

    def tail_part(p):
        query = [qsrc[p * PAIR + h] for h in range(PAIR)]
        cols = [head_cols(p * PAIR + h) for h in range(PAIR)]
        scores = []
        for r in range(req_here):
            s = jnp.concatenate(
                [matmul(tail[r, 0, :, cols[h]], query[h], ((1,), (1,))) for h in range(PAIR)], axis=1
            )
            token = lax.broadcasted_iota(jnp.int32, s.shape, 0)
            scores.append(jnp.where(token < tl_ref[r : r + 1, :], s, MASKED))
        s = jnp.concatenate(
            [matmul(fresh[0, :, cols[h]], query[h], ((1,), (1,))) for h in range(PAIR)], axis=1
        )
        token = lax.broadcasted_iota(jnp.int32, s.shape, 0)
        lane = lax.broadcasted_iota(jnp.int32, s.shape, 1)
        lane_step = lax.rem(lane // (GROUP * req_here), steps)
        live = (token < steps * req_here) & (lax.rem(token, req_here) == lax.rem(lane, req_here))
        live = live & (token // req_here <= lane_step)
        scores.append(jnp.where(live, s, MASKED))
        top, weights = attend(scores)
        total = functools.reduce(jnp.add, [jnp.sum(w, axis=0, keepdims=True) for w in weights])
        weights = [w.astype(jnp.bfloat16) for w in weights]
        stat = jnp.concatenate([top, total], axis=0)
        for h in range(PAIR):
            values = [tail[r, 1, :, cols[h]] for r in range(req_here)] + [fresh[1, :, cols[h]]]
            part = slice(h * rows, (h + 1) * rows)
            out = functools.reduce(
                jnp.add, [matmul(v, w[:, part], ((0,), (0,))) for v, w in zip(values, weights)]
            )
            tacc[p * PAIR + h] = jnp.concatenate([out[:half_dim], out[half_dim:]], axis=1)
            tst[p * PAIR + h] = jnp.concatenate([stat[:, part]] * 2, axis=1)

    def turn_values(c):
        cols = head_cols(c)
        for k in range(2):
            for b in range(n_root):
                i = k * n_root + b
                vt[c, :HD, i * block_len : (i + 1) * block_len] = root[k, b, 1, :, cols].T
            for b in range(n_branch):
                i = 2 * n_root + k * n_branch + b
                vt[c, :HD, i * block_len : (i + 1) * block_len] = branch[k, b, 1, :, cols].T

    def cache_parts(n):
        c = n // 2
        cols = head_cols(c)
        groups = 4
        span = vt.shape[2] // groups

        def keys(j):
            k = j % 2
            if j < 2:
                return jnp.concatenate([root[k, b, 0, :, cols] for b in range(n_root)], axis=0)
            key = jnp.concatenate([branch[k, b, 0, :, cols] for b in range(n_branch)], axis=0)
            mark = jnp.concatenate([kaug[k * n_branch + b] for b in range(n_branch)], axis=0)
            return jnp.concatenate([key, mark], axis=1)

        def queries(qbuf, y):
            query = jnp.concatenate([qbuf[n, z] for z in range(depth)], axis=0)
            first = lax.rem(n, 2) * depth
            mark = jnp.concatenate([qaug[y, first + z] for z in range(depth)], axis=0)
            return query, jnp.concatenate([query, mark], axis=1)

        def score(j, query):
            return matmul(keys(j), query[j // 2], ((1,), (1,)))

        query = queries(qfar, 1 - yy)
        scores = [score(j, query) for j in range(groups)]
        query = queries(qown, yy)
        for i in range(2):
            top = functools.reduce(
                jnp.maximum, [jnp.max(s, axis=0, keepdims=True) for s in scores]
            ) * UNIT
            later, out = [], None
            for j in range(groups):
                if i == 0:
                    later.append(score(j, query))
                w = jnp.exp2(scores[j] * UNIT - top).astype(jnp.bfloat16)
                part = matmul(vt[c, :, j * span : (j + 1) * span], w, ((1,), (0,)))
                out = part if out is None else out + part
            scores = later
            stat = jnp.concatenate([top, out[HD : HD + 1]], axis=0)
            if i == 0:
                put_o[n] = out[:HD].astype(jnp.bfloat16)
                put_s[n] = stat
                for copy in send_y(n):
                    copy.start()
            else:
                own_o[n] = out[:HD]
                own_s[n] = stat

    def merge(n):
        stat_a, stat_b = own_s[n], got_s[n]
        top = jnp.maximum(stat_a[0:1], stat_b[0:1])
        wa = jnp.exp2(stat_a[0:1] - top)
        wb = jnp.exp2(stat_b[0:1] - top)
        stat = jnp.concatenate([top, stat_a[1:2] * wa + stat_b[1:2] * wb], axis=0)
        out = own_o[n] * wa + got_o[n].astype(jnp.float32) * wb
        for z in range(depth):
            part = slice(z * rows, (z + 1) * rows)
            fold_o[n, z] = fold(out, part).astype(jnp.bfloat16)
            fold_s[n, z] = jnp.concatenate([stat[:, part]] * 2, axis=1)

    def finish(h):
        stats = [all_s[h, z] for z in range(depth)]
        own = tst[h]
        top = functools.reduce(jnp.maximum, [s[0:1] for s in stats] + [own[0:1]])
        scale = jnp.exp2(own[0:1] - top)
        number = tacc[h] * scale
        total = own[1:2] * scale
        for z in range(depth):
            factor = jnp.exp2(stats[z][0:1] - top)
            number = number + all_o[h, z].astype(jnp.float32) * factor
            total = total + stats[z][1:2] * factor
        out = number / total
        out = jnp.concatenate([out[:, :rows], out[:, rows:]], axis=0).T
        for s in range(steps):
            for g in range(GROUP):
                first = (s * GROUP + g) * req_here
                cols = pl.ds(pl.multiple_of((h * GROUP + g) * HD, HD), HD)
                out_ref[s, :, cols] = out[first : first + req_here].astype(jnp.bfloat16)

    tables()
    loads[2].wait()

    @pl.loop(0, chunks + LAG_LAST)
    def _(t):
        @pl.when(t < chunks)
        def _():
            gather_z_wait(t)
            gather_y(t).start()

        @pl.when((lax.rem(t, 2) == 1) & (t < 2 * (HEADS - AHEAD)))
        def _():
            gather_z_start(t // 2 + AHEAD)

        @pl.when(t < KVH // PAIR)
        def _():
            tail_part(t)

        @pl.when(t == LAG_WORK - 1)
        def _():
            for load in loads[:2]:
                load.wait()
            for share in shares_in:
                share.wait_recv()

        @pl.when((t >= LAG_WORK - 1) & (t < HEADS + LAG_WORK - 1))
        def _():
            turn_values(t - LAG_WORK + 1)

        @pl.when((t >= LAG_WORK) & (t < chunks + LAG_WORK))
        def _():
            n = t - LAG_WORK
            gather_y(n).wait_recv()
            cache_parts(n)

        @pl.when((t >= LAG_MERGE) & (t < chunks + LAG_MERGE))
        def _():
            n = t - LAG_MERGE
            for copy in send_y(n):
                copy.wait_recv()
            merge(n)
            for o in range(1, depth):
                for copy in send_z(n, lax.rem(zz + o, depth)):
                    copy.start()

            @pl.when(lax.rem(n, 2) != core)
            def _():
                for copy in send_z(n, zz):
                    copy.start()

            @pl.when(lax.rem(n, 2) == core)
            def _():
                all_o[core * HEADS + n // 2, zz] = fold_o[n, zz]
                all_s[core * HEADS + n // 2, zz] = fold_s[n, zz]

        for c in range(HEADS):

            @pl.when(t == 2 * c + core + LAG_LAST)
            def _(c=c):
                for k, first in ((core, 1), (1 - core, 0)):
                    h = k * HEADS + c
                    for o in range(first, depth):
                        for copy in send_z_in(h, lax.rem(zz + o, depth)):
                            copy.wait_recv()
                    finish(h)

    @pl.loop(0, HEADS)
    def _(c):
        for other in range(2):
            gather_z_sent(c, other).wait_send()

    @pl.loop(0, chunks)
    def _(n):
        gather_y(n).wait_send()
        for copy in send_y(n):
            copy.wait_send()

        @pl.when(lax.rem(n, 2) == core)
        def _():
            for copy in send_z_sent(n, depth - 1):
                copy.wait_send()

        @pl.when(lax.rem(n, 2) != core)
        def _():
            for copy in send_z_sent(n, depth):
                copy.wait_send()

    for share in shares:
        share.wait_send()


def body(queries, new_kv, root_kv, branch_kv, tail_kv, parent, node_len, leaf_of, branch_slot):
    devices = lax.axis_size("kv")
    steps, req_here, _ = queries.shape
    rows = steps * req_here * GROUP
    depth = devices // 4
    chunks = 2 * HEADS
    lanes = depth * rows
    n_root, _, block_len, _ = root_kv.shape
    n_branch = branch_kv.shape[0]
    tokens = 2 * (n_root + n_branch) * block_len
    bf, f32 = jnp.bfloat16, jnp.float32
    vmem = pl.BlockSpec(memory_space=pltpu.VMEM)
    smem = pl.BlockSpec(memory_space=pltpu.SMEM)
    hbm = pl.BlockSpec(memory_space=pl.ANY)
    dma = pltpu.SemaphoreType.DMA
    return pl.pallas_call(
        functools.partial(kernel, devices, steps, req_here),
        out_shape=jax.ShapeDtypeStruct(queries.shape, bf),
        in_specs=[smem] * 4 + [vmem] * 2 + [hbm] * 3,
        out_specs=vmem,
        scratch_shapes=[
            pltpu.VMEM((KVH, rows, HD), bf),
            pltpu.VMEM((chunks, depth, rows, HD), bf),
            pltpu.VMEM((chunks, depth, rows, HD), bf),
            pltpu.VMEM((2, n_root, 2, block_len, HEADS * HD), bf),
            pltpu.VMEM((2, n_branch, 2, block_len, HEADS * HD), bf),
            pltpu.VMEM(tail_kv.shape, bf),
            pltpu.VMEM((HEADS, HD + EXTRA, tokens), bf),
            pltpu.VMEM((2 * n_branch, block_len, HD), bf),
            pltpu.VMEM((2, depth * 2, rows, HD), bf),
            pltpu.VMEM((req_here, PAIR * rows), jnp.int32),
            pltpu.VMEM((2, 16, KVH * HD), bf),
            pltpu.VMEM((chunks, HD, lanes), f32),
            pltpu.VMEM((chunks, 2, lanes), f32),
            pltpu.VMEM((chunks, HD, lanes), bf),
            pltpu.VMEM((chunks, 2, lanes), f32),
            pltpu.VMEM((chunks, HD, lanes), bf),
            pltpu.VMEM((chunks, 2, lanes), f32),
            pltpu.VMEM((chunks, depth, HD // 2, 2 * rows), bf),
            pltpu.VMEM((chunks, depth, 2, 2 * rows), f32),
            pltpu.VMEM((KVH, depth, HD // 2, 2 * rows), bf),
            pltpu.VMEM((KVH, depth, 2, 2 * rows), f32),
            pltpu.VMEM((KVH, HD // 2, 2 * rows), f32),
            pltpu.VMEM((KVH, 2, 2 * rows), f32),
            dma((3,)), dma((2,)), dma((2,)),
            dma((HEADS, 2)), dma((chunks, depth)), dma((chunks,)), dma((chunks,)),
            dma((chunks, 2)), dma((chunks, 2)), dma((chunks, 2)), dma((KVH, depth, 2)),
        ],
        compiler_params=pltpu.CompilerParams(
            collective_id=0, has_side_effects=True, vmem_limit_bytes=56 * 1024 * 1024
        ),
    )(parent, node_len, leaf_of, branch_slot, queries, new_kv, root_kv, branch_kv, tail_kv)


def solution(mesh):
    return jax.shard_map(
        body,
        mesh=mesh,
        in_specs=(
            P(None, ("groups", "kv"), None),
            P(None, None, ("groups", "kv"), None),
            P(("groups", "kv"), None, None, None),
            P(("groups", "kv"), None, None, None),
            P(("groups", "kv"), None, None, None),
            P("groups"),
            P("groups"),
            P("groups"),
            P("groups"),
        ),
        out_specs=P(None, ("groups", "kv"), None),
        check_vma=False,
    )
```

```python
import functools

import jax
import jax.numpy as jnp
from jax import lax
from jax.experimental import pallas as pl
from jax.experimental.pallas import tpu as pltpu
from jax.sharding import PartitionSpec as P

QH = 128
KVH = 8
HD = 128
GROUP = QH // KVH
HEADS = KVH // 2
PAIR = 2
MASKED = -1e30
UNIT = HD**-0.5 * 1.4426950408889634
EXTRA = 16
LAG_WORK = 2
LAG_MERGE = 4
LAG_LAST = 6


def matmul(a, b, dims):
    return lax.dot_general(a, b, (dims, ((), ())), preferred_element_type=jnp.float32)


def attend(scores):
    top = functools.reduce(jnp.maximum, [jnp.max(s, axis=0, keepdims=True) for s in scores]) * UNIT
    weights = [jnp.exp2(s * UNIT - top) for s in scores]
    return top, weights


def kernel(
    devices, steps, req_here,
    parent, node_len, leaf_of, branch_slot,
    q_in, new_ref, root_hbm, branch_hbm, tail_hbm,
    out_ref,
    qsrc, qown, qfar, root, branch, tail, vt, kaug, qaug, tl_ref, fresh,
    own_o, own_s, put_o, put_s, got_o, got_s, fold_o, fold_s, all_o, all_s, tacc, tst,
    hbm_sem, kv_s, kv_r, gz_s, gz_r, gy_s, gy_r, y_s, y_r, z_s, z_r,
):
    depth = devices // 4
    rows = steps * req_here * GROUP
    chunks = 2 * HEADS
    lanes = depth * rows
    half_dim = HD // 2
    me = lax.axis_index("kv")
    core = lax.rem(me, 2)
    yy = lax.rem(me // 2, 2)
    zz = me // 4
    core_peer = me + 1 - 2 * core
    y_peer = me + 2 - 4 * yy
    n_root = root.shape[1]
    n_branch = branch.shape[1]
    block_len = root.shape[3]
    blocks = 2 * (n_root + n_branch)
    half_cols = HEADS * HD

    def device(z, k):
        return z * 4 + yy * 2 + k

    def remote(src, dst, send, recv, peer):
        return pltpu.make_async_remote_copy(
            src_ref=src, dst_ref=dst, send_sem=send, recv_sem=recv,
            device_id={"kv": peer}, device_id_type=pl.DeviceIdType.MESH,
        )

    def half(ref, k):
        return ref.at[:, :, :, pl.ds(pl.multiple_of(k * half_cols, half_cols), half_cols)]

    loads = [
        pltpu.make_async_copy(half(root_hbm, core), root.at[core], hbm_sem.at[0]),
        pltpu.make_async_copy(half(branch_hbm, core), branch.at[core], hbm_sem.at[1]),
        pltpu.make_async_copy(tail_hbm, tail, hbm_sem.at[2]),
    ]
    shares = [
        remote(half(root_hbm, 1 - core), root.at[core], kv_s.at[0], kv_r.at[0], core_peer),
        remote(half(branch_hbm, 1 - core), branch.at[core], kv_s.at[1], kv_r.at[1], core_peer),
    ]
    shares_in = [
        remote(root.at[core], root.at[1 - core], kv_s.at[0], kv_r.at[0], core_peer),
        remote(branch.at[core], branch.at[1 - core], kv_s.at[1], kv_r.at[1], core_peer),
    ]
    for load in loads:
        load.start()

    barrier = pltpu.get_barrier_semaphore()
    peers = [core_peer, y_peer]
    for o in range(1, depth):
        z = lax.rem(zz + o, depth)
        peers += [device(z, core), device(z, 1 - core)]
    for peer in peers:
        pl.semaphore_signal(
            barrier, inc=1, device_id={"kv": peer}, device_id_type=pl.DeviceIdType.MESH
        )

    def lay_out(h):
        pieces = []
        for s in range(steps):
            for g in range(GROUP):
                cols = pl.ds(pl.multiple_of((h * GROUP + g) * HD, HD), HD)
                pieces.append(q_in[s, :, cols].astype(jnp.float32))
        qsrc[h] = jnp.concatenate(pieces, axis=0).astype(jnp.bfloat16)

    @pl.loop(0, KVH)
    def _(h):
        lay_out(h)

    pl.semaphore_wait(barrier, len(peers))

    def gather_z_start(c):
        dst = qown.at[c * 2 + core, zz]
        for k in (core, 1 - core):
            for o in range(depth - 1, 0, -1):
                z = lax.rem(zz + o, depth)
                gather_z(c, k, dst, device(z, k)).start()
        gather_z(c, 1 - core, dst, core_peer).start()
        qown[c * 2 + core, zz] = qsrc[core * HEADS + c]

    def gather_z(c, k, dst, peer):
        return remote(
            qsrc.at[k * HEADS + c], dst, gz_s.at[c, lax.rem(k + core, 2)],
            gz_r.at[c * 2 + core], peer,
        )

    gather_z_start(0)
    for share in shares:
        share.start()

    def gather_z_wait(n):
        def wait(count):
            part = qown.at[n, pl.ds(0, count)]
            remote(part, part, gz_s.at[0, 0], gz_r.at[n], y_peer).wait_recv()

        @pl.when(lax.rem(n, 2) == core)
        def _():
            wait(depth - 1)

        @pl.when(lax.rem(n, 2) != core)
        def _():
            wait(depth)

    def gather_z_sent(c):
        for other in range(2):
            part = qown.at[0, pl.ds(0, depth - 1 + other)]
            remote(part, part, gz_s.at[c, other], gz_r.at[0], y_peer).wait_send()

    def gather_y(n):
        return remote(qown.at[n], qfar.at[n], gy_s.at[n], gy_r.at[n], y_peer)

    def send_y(n):
        return (
            remote(put_o.at[n], got_o.at[n], y_s.at[n, 0], y_r.at[n, 0], y_peer),
            remote(put_s.at[n], got_s.at[n], y_s.at[n, 1], y_r.at[n, 1], y_peer),
        )

    def send_z(n, z):
        c = n // 2
        h = core * HEADS + c
        peer = device(z, lax.rem(n, 2))
        return (
            remote(fold_o.at[n, z], all_o.at[h, zz], z_s.at[n, 0], z_r.at[h, 0], peer),
            remote(fold_s.at[n, z], all_s.at[h, zz], z_s.at[n, 1], z_r.at[h, 1], peer),
        )

    def send_z_in(h, count):
        part = pl.ds(0, count)
        return (
            remote(all_o.at[h, part], all_o.at[h, part], z_s.at[0, 0], z_r.at[h, 0], y_peer),
            remote(all_s.at[h, part], all_s.at[h, part], z_s.at[0, 1], z_r.at[h, 1], y_peer),
        )

    def send_z_sent(n, count):
        part = pl.ds(0, count)
        return (
            remote(fold_o.at[n, part], fold_o.at[n, part], z_s.at[n, 0], z_r.at[0, 0], y_peer),
            remote(fold_s.at[n, part], fold_s.at[n, part], z_s.at[n, 1], z_r.at[0, 1], y_peer),
        )

    def tables():
        slots = 2 * n_branch
        first_slot = (me // 2) * slots
        slot_nodes = [branch_slot[first_slot + j] for j in range(slots)]

        def count_rank(i, ranks):
            node = branch_slot[i]
            return tuple(
                rank + jnp.where((node == slot_nodes[j]) & (i < first_slot + j), 1, 0)
                for j, rank in enumerate(ranks)
            )

        ranks = lax.fori_loop(0, branch_slot.shape[0], count_rank, (jnp.int32(0),) * slots)
        token = lax.broadcasted_iota(jnp.int32, (block_len, HD), 0)
        lane = lax.broadcasted_iota(jnp.int32, (block_len, HD), 1)
        for j in range(slots):
            owned = node_len[jnp.minimum(slot_nodes[j], node_len.shape[0] - 1)]
            fill = jnp.clip(owned - ranks[j] * block_len, 0, block_len)
            fill = jnp.where(slot_nodes[j] < node_len.shape[0], fill, 0)
            x = jnp.where(lane == j, 1.0, 0.0)
            x = jnp.where((lane == slots) & (token >= fill), MASKED, x)
            kaug[j] = x.astype(jnp.bfloat16)
        tile = 16
        lane = lax.broadcasted_iota(jnp.int32, (tile, HD), 1)
        which = lax.rem(lax.broadcasted_iota(jnp.int32, (tile, HD), 0), req_here)
        slot_of_lane = jnp.full((tile, HD), -1, jnp.int32)
        for j in range(slots):
            slot_of_lane = jnp.where(lane == j, slot_nodes[j], slot_of_lane)
        for y in range(2):
            for i in range(2 * depth):
                owner = (i % depth) * 4 + y * 2 + i // depth
                node = jnp.zeros((tile, HD), jnp.int32)
                for r in range(req_here):
                    node = jnp.where(which == r, parent[leaf_of[owner * req_here + r]], node)
                x = jnp.where(node == slot_of_lane, 0.0, MASKED)
                x = jnp.where(lane < slots, x, jnp.where(lane == slots, 1.0, 0.0))
                qaug[y, i] = jnp.concatenate([x] * (rows // tile), axis=0).astype(jnp.bfloat16)
        lane = lax.broadcasted_iota(jnp.int32, (1, PAIR * rows), 1)
        for r in range(req_here):
            tl_ref[r : r + 1, :] = jnp.where(
                lax.rem(lane, req_here) == r, node_len[leaf_of[me * req_here + r]], 0
            )
        fresh[...] = jnp.zeros_like(fresh)
        for s in range(steps):
            for kv in range(2):
                fresh[kv, s * req_here : (s + 1) * req_here, :] = new_ref[s, kv]
        vt[:, HD:, :] = jnp.ones((HEADS, EXTRA, vt.shape[2]), jnp.bfloat16)

    def head_cols(k):
        return pl.ds(pl.multiple_of(k * HD, HD), HD)

    def fold(x, part):
        return jnp.concatenate([x[:half_dim, part], x[half_dim:, part]], axis=1)

    def tail_part(p):
        query = [qsrc[p * PAIR + h] for h in range(PAIR)]
        cols = [head_cols(p * PAIR + h) for h in range(PAIR)]
        scores = []
        for r in range(req_here):
            s = jnp.concatenate(
                [matmul(tail[r, 0, :, cols[h]], query[h], ((1,), (1,))) for h in range(PAIR)], axis=1
            )
            token = lax.broadcasted_iota(jnp.int32, s.shape, 0)
            scores.append(jnp.where(token < tl_ref[r : r + 1, :], s, MASKED))
        s = jnp.concatenate(
            [matmul(fresh[0, :, cols[h]], query[h], ((1,), (1,))) for h in range(PAIR)], axis=1
        )
        token = lax.broadcasted_iota(jnp.int32, s.shape, 0)
        lane = lax.broadcasted_iota(jnp.int32, s.shape, 1)
        lane_step = lax.rem(lane // (GROUP * req_here), steps)
        live = (token < steps * req_here) & (lax.rem(token, req_here) == lax.rem(lane, req_here))
        live = live & (token // req_here <= lane_step)
        scores.append(jnp.where(live, s, MASKED))
        top, weights = attend(scores)
        total = functools.reduce(jnp.add, [jnp.sum(w, axis=0, keepdims=True) for w in weights])
        weights = [w.astype(jnp.bfloat16) for w in weights]
        stat = jnp.concatenate([top, total], axis=0)
        for h in range(PAIR):
            values = [tail[r, 1, :, cols[h]] for r in range(req_here)] + [fresh[1, :, cols[h]]]
            part = slice(h * rows, (h + 1) * rows)
            out = functools.reduce(
                jnp.add, [matmul(v, w[:, part], ((0,), (0,))) for v, w in zip(values, weights)]
            )
            tacc[p * PAIR + h] = jnp.concatenate([out[:half_dim], out[half_dim:]], axis=1)
            tst[p * PAIR + h] = jnp.concatenate([stat[:, part]] * 2, axis=1)

    def turn_values(c):
        cols = head_cols(c)
        for k in range(2):
            for b in range(n_root):
                i = k * n_root + b
                vt[c, :HD, i * block_len : (i + 1) * block_len] = root[k, b, 1, :, cols].T
            for b in range(n_branch):
                i = 2 * n_root + k * n_branch + b
                vt[c, :HD, i * block_len : (i + 1) * block_len] = branch[k, b, 1, :, cols].T

    def cache_parts(n):
        c = n // 2
        cols = head_cols(c)
        groups = 4
        span = vt.shape[2] // groups

        def keys(j):
            k = j % 2
            if j < 2:
                return jnp.concatenate([root[k, b, 0, :, cols] for b in range(n_root)], axis=0)
            key = jnp.concatenate([branch[k, b, 0, :, cols] for b in range(n_branch)], axis=0)
            mark = jnp.concatenate([kaug[k * n_branch + b] for b in range(n_branch)], axis=0)
            return jnp.concatenate([key, mark], axis=1)

        def queries(qbuf, y):
            query = jnp.concatenate([qbuf[n, z] for z in range(depth)], axis=0)
            first = lax.rem(n, 2) * depth
            mark = jnp.concatenate([qaug[y, first + z] for z in range(depth)], axis=0)
            return query, jnp.concatenate([query, mark], axis=1)

        def score(j, query):
            return matmul(keys(j), query[j // 2], ((1,), (1,)))

        query = queries(qfar, 1 - yy)
        scores = [score(j, query) for j in range(groups)]
        query = queries(qown, yy)
        for i in range(2):
            top = functools.reduce(
                jnp.maximum, [jnp.max(s, axis=0, keepdims=True) for s in scores]
            ) * UNIT
            later, out = [], None
            for j in range(groups):
                if i == 0:
                    later.append(score(j, query))
                w = jnp.exp2(scores[j] * UNIT - top).astype(jnp.bfloat16)
                part = matmul(vt[c, :, j * span : (j + 1) * span], w, ((1,), (0,)))
                out = part if out is None else out + part
            scores = later
            stat = jnp.concatenate([top, out[HD : HD + 1]], axis=0)
            if i == 0:
                put_o[n] = out[:HD].astype(jnp.bfloat16)
                put_s[n] = stat
                for copy in send_y(n):
                    copy.start()
            else:
                own_o[n] = out[:HD]
                own_s[n] = stat

    def merge(n):
        stat_a, stat_b = own_s[n], got_s[n]
        top = jnp.maximum(stat_a[0:1], stat_b[0:1])
        wa = jnp.exp2(stat_a[0:1] - top)
        wb = jnp.exp2(stat_b[0:1] - top)
        stat = jnp.concatenate([top, stat_a[1:2] * wa + stat_b[1:2] * wb], axis=0)
        out = own_o[n] * wa + got_o[n].astype(jnp.float32) * wb
        for z in range(depth):
            part = slice(z * rows, (z + 1) * rows)
            fold_o[n, z] = fold(out, part).astype(jnp.bfloat16)
            fold_s[n, z] = jnp.concatenate([stat[:, part]] * 2, axis=1)

    def finish(h):
        stats = [all_s[h, z] for z in range(depth)]
        own = tst[h]
        top = functools.reduce(jnp.maximum, [s[0:1] for s in stats] + [own[0:1]])
        scale = jnp.exp2(own[0:1] - top)
        number = tacc[h] * scale
        total = own[1:2] * scale
        for z in range(depth):
            factor = jnp.exp2(stats[z][0:1] - top)
            number = number + all_o[h, z].astype(jnp.float32) * factor
            total = total + stats[z][1:2] * factor
        out = number / total
        out = jnp.concatenate([out[:, :rows], out[:, rows:]], axis=0).T
        for s in range(steps):
            for g in range(GROUP):
                first = (s * GROUP + g) * req_here
                cols = pl.ds(pl.multiple_of((h * GROUP + g) * HD, HD), HD)
                out_ref[s, :, cols] = out[first : first + req_here].astype(jnp.bfloat16)

    tables()
    gather_z_sent(0)
    gather_z_start(1)
    loads[2].wait()

    @pl.loop(0, chunks + LAG_LAST)
    def _(t):
        @pl.when(t < chunks)
        def _():
            gather_z_wait(t)
            gather_y(t).start()

        @pl.when(t < KVH // PAIR)
        def _():
            tail_part(t)

        @pl.when((lax.rem(t, 2) == 1) & (t < 2 * (HEADS - 2)))
        def _():
            gather_z_sent(t // 2 + 1)
            gather_z_start(t // 2 + 2)

        @pl.when(t == LAG_WORK - 1)
        def _():
            for load in loads[:2]:
                load.wait()
            for share in shares_in:
                share.wait_recv()

        @pl.when((t >= LAG_WORK - 1) & (t < HEADS + LAG_WORK - 1))
        def _():
            turn_values(t - LAG_WORK + 1)

        @pl.when((t >= LAG_WORK) & (t < chunks + LAG_WORK))
        def _():
            n = t - LAG_WORK
            gather_y(n).wait_recv()
            cache_parts(n)

        @pl.when((t >= LAG_MERGE) & (t < chunks + LAG_MERGE))
        def _():
            n = t - LAG_MERGE
            for copy in send_y(n):
                copy.wait_recv()
            merge(n)
            for o in range(1, depth):
                for copy in send_z(n, lax.rem(zz + o, depth)):
                    copy.start()

            @pl.when(lax.rem(n, 2) != core)
            def _():
                for copy in send_z(n, zz):
                    copy.start()

            @pl.when(lax.rem(n, 2) == core)
            def _():
                all_o[core * HEADS + n // 2, zz] = fold_o[n, zz]
                all_s[core * HEADS + n // 2, zz] = fold_s[n, zz]

        for c in range(HEADS):

            @pl.when(t == 2 * c + core + LAG_LAST)
            def _(c=c):
                for k, count in ((core, depth - 1), (1 - core, depth)):
                    h = k * HEADS + c
                    for copy in send_z_in(h, count):
                        copy.wait_recv()
                    finish(h)

    gather_z_sent(HEADS - 1)

    @pl.loop(0, chunks)
    def _(n):
        gather_y(n).wait_send()
        for copy in send_y(n):
            copy.wait_send()

        @pl.when(lax.rem(n, 2) == core)
        def _():
            for copy in send_z_sent(n, depth - 1):
                copy.wait_send()

        @pl.when(lax.rem(n, 2) != core)
        def _():
            for copy in send_z_sent(n, depth):
                copy.wait_send()

    for share in shares:
        share.wait_send()


def body(queries, new_kv, root_kv, branch_kv, tail_kv, parent, node_len, leaf_of, branch_slot):
    devices = lax.axis_size("kv")
    steps, req_here, _ = queries.shape
    rows = steps * req_here * GROUP
    depth = devices // 4
    chunks = 2 * HEADS
    lanes = depth * rows
    n_root, _, block_len, _ = root_kv.shape
    n_branch = branch_kv.shape[0]
    tokens = 2 * (n_root + n_branch) * block_len
    bf, f32 = jnp.bfloat16, jnp.float32
    vmem = pl.BlockSpec(memory_space=pltpu.VMEM)
    smem = pl.BlockSpec(memory_space=pltpu.SMEM)
    hbm = pl.BlockSpec(memory_space=pl.ANY)
    dma = pltpu.SemaphoreType.DMA
    return pl.pallas_call(
        functools.partial(kernel, devices, steps, req_here),
        out_shape=jax.ShapeDtypeStruct(queries.shape, bf),
        in_specs=[smem] * 4 + [vmem] * 2 + [hbm] * 3,
        out_specs=vmem,
        scratch_shapes=[
            pltpu.VMEM((KVH, rows, HD), bf),
            pltpu.VMEM((chunks, depth, rows, HD), bf),
            pltpu.VMEM((chunks, depth, rows, HD), bf),
            pltpu.VMEM((2, n_root, 2, block_len, HEADS * HD), bf),
            pltpu.VMEM((2, n_branch, 2, block_len, HEADS * HD), bf),
            pltpu.VMEM(tail_kv.shape, bf),
            pltpu.VMEM((HEADS, HD + EXTRA, tokens), bf),
            pltpu.VMEM((2 * n_branch, block_len, HD), bf),
            pltpu.VMEM((2, depth * 2, rows, HD), bf),
            pltpu.VMEM((req_here, PAIR * rows), jnp.int32),
            pltpu.VMEM((2, 16, KVH * HD), bf),
            pltpu.VMEM((chunks, HD, lanes), f32),
            pltpu.VMEM((chunks, 2, lanes), f32),
            pltpu.VMEM((chunks, HD, lanes), bf),
            pltpu.VMEM((chunks, 2, lanes), f32),
            pltpu.VMEM((chunks, HD, lanes), bf),
            pltpu.VMEM((chunks, 2, lanes), f32),
            pltpu.VMEM((chunks, depth, HD // 2, 2 * rows), bf),
            pltpu.VMEM((chunks, depth, 2, 2 * rows), f32),
            pltpu.VMEM((KVH, depth, HD // 2, 2 * rows), bf),
            pltpu.VMEM((KVH, depth, 2, 2 * rows), f32),
            pltpu.VMEM((KVH, HD // 2, 2 * rows), f32),
            pltpu.VMEM((KVH, 2, 2 * rows), f32),
            dma((3,)), dma((2,)), dma((2,)),
            dma((HEADS, 2)), dma((chunks,)), dma((chunks,)), dma((chunks,)),
            dma((chunks, 2)), dma((chunks, 2)), dma((chunks, 2)), dma((KVH, 2)),
        ],
        compiler_params=pltpu.CompilerParams(
            collective_id=0, has_side_effects=True, vmem_limit_bytes=56 * 1024 * 1024
        ),
    )(parent, node_len, leaf_of, branch_slot, queries, new_kv, root_kv, branch_kv, tail_kv)


def solution(mesh):
    return jax.shard_map(
        body,
        mesh=mesh,
        in_specs=(
            P(None, ("groups", "kv"), None),
            P(None, None, ("groups", "kv"), None),
            P(("groups", "kv"), None, None, None),
            P(("groups", "kv"), None, None, None),
            P(("groups", "kv"), None, None, None),
            P("groups"),
            P("groups"),
            P("groups"),
            P("groups"),
        ),
        out_specs=P(None, ("groups", "kv"), None),
        check_vma=False,
    )
```

```python
import functools

import jax
import jax.numpy as jnp
from jax import lax
from jax.experimental import pallas as pl
from jax.experimental.pallas import tpu as pltpu
from jax.sharding import PartitionSpec as P

QH = 128
KVH = 8
HD = 128
GROUP = QH // KVH
HEADS = KVH // 2
PAIR = 2
MASKED = -1e30
UNIT = HD**-0.5 * 1.4426950408889634
EXTRA = 16
LAG_WORK = 2
LAG_MERGE = 4
LAG_LAST = 6


def matmul(a, b, dims):
    return lax.dot_general(a, b, (dims, ((), ())), preferred_element_type=jnp.float32)


def attend(scores):
    top = functools.reduce(jnp.maximum, [jnp.max(s, axis=0, keepdims=True) for s in scores]) * UNIT
    weights = [jnp.exp2(s * UNIT - top) for s in scores]
    return top, weights


def kernel(
    devices, steps, req_here,
    parent_hbm, node_len_hbm, leaf_hbm, slot_hbm,
    q_hbm, new_hbm, root_hbm, branch_hbm, tail_hbm,
    out_ref,
    parent, node_len, leaf_of, branch_slot, q_in, new_ref, qsrc, qown, qfar, root, branch, tail, vt, kaug, qaug, tl_ref, fresh,
    own_o, own_s, put_o, put_s, got_o, got_s, fold_o, fold_s, all_o, all_s, tacc, tst,
    hbm_sem, kv_s, kv_r, gz_s, gz_r, gy_s, gy_r, y_s, y_r, z_s, z_r,
):
    depth = devices // 4
    rows = steps * req_here * GROUP
    chunks = 2 * HEADS
    lanes = depth * rows
    half_dim = HD // 2
    me = lax.axis_index("kv")
    core = lax.rem(me, 2)
    yy = lax.rem(me // 2, 2)
    zz = me // 4
    core_peer = me + 1 - 2 * core
    y_peer = me + 2 - 4 * yy
    n_root = root.shape[1]
    n_branch = branch.shape[1]
    block_len = root.shape[3]
    blocks = 2 * (n_root + n_branch)
    half_cols = HEADS * HD

    def device(z, k):
        return z * 4 + yy * 2 + k

    def remote(src, dst, send, recv, peer):
        return pltpu.make_async_remote_copy(
            src_ref=src, dst_ref=dst, send_sem=send, recv_sem=recv,
            device_id={"kv": peer}, device_id_type=pl.DeviceIdType.MESH,
        )

    def half(ref, k):
        return ref.at[:, :, :, pl.ds(pl.multiple_of(k * half_cols, half_cols), half_cols)]

    first_loads = [
        pltpu.make_async_copy(q_hbm, q_in, hbm_sem.at[3]),
        pltpu.make_async_copy(new_hbm, new_ref, hbm_sem.at[4]),
    ]
    table_loads = [
        pltpu.make_async_copy(parent_hbm, parent, hbm_sem.at[5]),
        pltpu.make_async_copy(node_len_hbm, node_len, hbm_sem.at[6]),
        pltpu.make_async_copy(leaf_hbm, leaf_of, hbm_sem.at[7]),
        pltpu.make_async_copy(slot_hbm, branch_slot, hbm_sem.at[8]),
    ]
    loads = [
        pltpu.make_async_copy(half(root_hbm, core), root.at[core], hbm_sem.at[0]),
        pltpu.make_async_copy(half(branch_hbm, core), branch.at[core], hbm_sem.at[1]),
        pltpu.make_async_copy(tail_hbm, tail, hbm_sem.at[2]),
    ]
    shares = [
        remote(half(root_hbm, 1 - core), root.at[core], kv_s.at[0], kv_r.at[0], core_peer),
        remote(half(branch_hbm, 1 - core), branch.at[core], kv_s.at[1], kv_r.at[1], core_peer),
    ]
    shares_in = [
        remote(root.at[core], root.at[1 - core], kv_s.at[0], kv_r.at[0], core_peer),
        remote(branch.at[core], branch.at[1 - core], kv_s.at[1], kv_r.at[1], core_peer),
    ]
    for load in first_loads + table_loads + loads:
        load.start()

    barrier = pltpu.get_barrier_semaphore()
    peers = [core_peer, y_peer]
    for o in range(1, depth):
        z = lax.rem(zz + o, depth)
        peers += [device(z, core), device(z, 1 - core)]
    for peer in peers:
        pl.semaphore_signal(
            barrier, inc=1, device_id={"kv": peer}, device_id_type=pl.DeviceIdType.MESH
        )

    def lay_out(h):
        pieces = []
        for s in range(steps):
            for g in range(GROUP):
                cols = pl.ds(pl.multiple_of((h * GROUP + g) * HD, HD), HD)
                pieces.append(q_in[s, :, cols].astype(jnp.float32))
        qsrc[h] = jnp.concatenate(pieces, axis=0).astype(jnp.bfloat16)

    for load in first_loads:
        load.wait()

    @pl.loop(0, KVH)
    def _(h):
        lay_out(h)

    pl.semaphore_wait(barrier, len(peers))

    def gather_z_start(c):
        dst = qown.at[c * 2 + core, zz]
        for k in (core, 1 - core):
            for o in range(depth - 1, 0, -1):
                z = lax.rem(zz + o, depth)
                gather_z(c, k, dst, device(z, k)).start()
        gather_z(c, 1 - core, dst, core_peer).start()
        qown[c * 2 + core, zz] = qsrc[core * HEADS + c]

    def gather_z(c, k, dst, peer):
        return remote(
            qsrc.at[k * HEADS + c], dst, gz_s.at[c, lax.rem(k + core, 2)],
            gz_r.at[c * 2 + core], peer,
        )

    gather_z_start(0)
    for share in shares:
        share.start()

    def gather_z_wait(n):
        def wait(count):
            part = qown.at[n, pl.ds(0, count)]
            remote(part, part, gz_s.at[0, 0], gz_r.at[n], y_peer).wait_recv()

        @pl.when(lax.rem(n, 2) == core)
        def _():
            wait(depth - 1)

        @pl.when(lax.rem(n, 2) != core)
        def _():
            wait(depth)

    def gather_z_sent(c):
        for other in range(2):
            part = qown.at[0, pl.ds(0, depth - 1 + other)]
            remote(part, part, gz_s.at[c, other], gz_r.at[0], y_peer).wait_send()

    def gather_y(n):
        return remote(qown.at[n], qfar.at[n], gy_s.at[n], gy_r.at[n], y_peer)

    def send_y(n):
        return (
            remote(put_o.at[n], got_o.at[n], y_s.at[n, 0], y_r.at[n, 0], y_peer),
            remote(put_s.at[n], got_s.at[n], y_s.at[n, 1], y_r.at[n, 1], y_peer),
        )

    def send_z(n, z):
        c = n // 2
        h = core * HEADS + c
        peer = device(z, lax.rem(n, 2))
        return (
            remote(fold_o.at[n, z], all_o.at[h, zz], z_s.at[n, 0], z_r.at[h, 0], peer),
            remote(fold_s.at[n, z], all_s.at[h, zz], z_s.at[n, 1], z_r.at[h, 1], peer),
        )

    def send_z_in(h, count):
        part = pl.ds(0, count)
        return (
            remote(all_o.at[h, part], all_o.at[h, part], z_s.at[0, 0], z_r.at[h, 0], y_peer),
            remote(all_s.at[h, part], all_s.at[h, part], z_s.at[0, 1], z_r.at[h, 1], y_peer),
        )

    def send_z_sent(n, count):
        part = pl.ds(0, count)
        return (
            remote(fold_o.at[n, part], fold_o.at[n, part], z_s.at[n, 0], z_r.at[0, 0], y_peer),
            remote(fold_s.at[n, part], fold_s.at[n, part], z_s.at[n, 1], z_r.at[0, 1], y_peer),
        )

    def tables():
        slots = 2 * n_branch
        first_slot = (me // 2) * slots
        slot_nodes = [branch_slot[first_slot + j] for j in range(slots)]

        def count_rank(i, ranks):
            node = branch_slot[i]
            return tuple(
                rank + jnp.where((node == slot_nodes[j]) & (i < first_slot + j), 1, 0)
                for j, rank in enumerate(ranks)
            )

        ranks = lax.fori_loop(0, branch_slot.shape[0], count_rank, (jnp.int32(0),) * slots)
        token = lax.broadcasted_iota(jnp.int32, (block_len, HD), 0)
        lane = lax.broadcasted_iota(jnp.int32, (block_len, HD), 1)
        for j in range(slots):
            owned = node_len[jnp.minimum(slot_nodes[j], node_len.shape[0] - 1)]
            fill = jnp.clip(owned - ranks[j] * block_len, 0, block_len)
            fill = jnp.where(slot_nodes[j] < node_len.shape[0], fill, 0)
            x = jnp.where(lane == j, 1.0, 0.0)
            x = jnp.where((lane == slots) & (token >= fill), MASKED, x)
            kaug[j] = x.astype(jnp.bfloat16)
        tile = 16
        lane = lax.broadcasted_iota(jnp.int32, (tile, HD), 1)
        which = lax.rem(lax.broadcasted_iota(jnp.int32, (tile, HD), 0), req_here)
        slot_of_lane = jnp.full((tile, HD), -1, jnp.int32)
        for j in range(slots):
            slot_of_lane = jnp.where(lane == j, slot_nodes[j], slot_of_lane)
        for y in range(2):
            for i in range(2 * depth):
                owner = (i % depth) * 4 + y * 2 + i // depth
                node = jnp.zeros((tile, HD), jnp.int32)
                for r in range(req_here):
                    node = jnp.where(which == r, parent[leaf_of[owner * req_here + r]], node)
                x = jnp.where(node == slot_of_lane, 0.0, MASKED)
                x = jnp.where(lane < slots, x, jnp.where(lane == slots, 1.0, 0.0))
                qaug[y, i] = jnp.concatenate([x] * (rows // tile), axis=0).astype(jnp.bfloat16)
        lane = lax.broadcasted_iota(jnp.int32, (1, PAIR * rows), 1)
        for r in range(req_here):
            tl_ref[r : r + 1, :] = jnp.where(
                lax.rem(lane, req_here) == r, node_len[leaf_of[me * req_here + r]], 0
            )
        fresh[...] = jnp.zeros_like(fresh)
        for s in range(steps):
            for kv in range(2):
                fresh[kv, s * req_here : (s + 1) * req_here, :] = new_ref[s, kv]
        vt[:, HD:, :] = jnp.ones((HEADS, EXTRA, vt.shape[2]), jnp.bfloat16)

    def head_cols(k):
        return pl.ds(pl.multiple_of(k * HD, HD), HD)

    def fold(x, part):
        return jnp.concatenate([x[:half_dim, part], x[half_dim:, part]], axis=1)

    def tail_part(p):
        query = [qsrc[p * PAIR + h] for h in range(PAIR)]
        cols = [head_cols(p * PAIR + h) for h in range(PAIR)]
        scores = []
        for r in range(req_here):
            s = jnp.concatenate(
                [matmul(tail[r, 0, :, cols[h]], query[h], ((1,), (1,))) for h in range(PAIR)], axis=1
            )
            token = lax.broadcasted_iota(jnp.int32, s.shape, 0)
            scores.append(jnp.where(token < tl_ref[r : r + 1, :], s, MASKED))
        s = jnp.concatenate(
            [matmul(fresh[0, :, cols[h]], query[h], ((1,), (1,))) for h in range(PAIR)], axis=1
        )
        token = lax.broadcasted_iota(jnp.int32, s.shape, 0)
        lane = lax.broadcasted_iota(jnp.int32, s.shape, 1)
        lane_step = lax.rem(lane // (GROUP * req_here), steps)
        live = (token < steps * req_here) & (lax.rem(token, req_here) == lax.rem(lane, req_here))
        live = live & (token // req_here <= lane_step)
        scores.append(jnp.where(live, s, MASKED))
        top, weights = attend(scores)
        total = functools.reduce(jnp.add, [jnp.sum(w, axis=0, keepdims=True) for w in weights])
        weights = [w.astype(jnp.bfloat16) for w in weights]
        stat = jnp.concatenate([top, total], axis=0)
        for h in range(PAIR):
            values = [tail[r, 1, :, cols[h]] for r in range(req_here)] + [fresh[1, :, cols[h]]]
            part = slice(h * rows, (h + 1) * rows)
            out = functools.reduce(
                jnp.add, [matmul(v, w[:, part], ((0,), (0,))) for v, w in zip(values, weights)]
            )
            tacc[p * PAIR + h] = jnp.concatenate([out[:half_dim], out[half_dim:]], axis=1)
            tst[p * PAIR + h] = jnp.concatenate([stat[:, part]] * 2, axis=1)

    def turn_values(c):
        cols = head_cols(c)
        for k in range(2):
            for b in range(n_root):
                i = k * n_root + b
                vt[c, :HD, i * block_len : (i + 1) * block_len] = root[k, b, 1, :, cols].T
            for b in range(n_branch):
                i = 2 * n_root + k * n_branch + b
                vt[c, :HD, i * block_len : (i + 1) * block_len] = branch[k, b, 1, :, cols].T

    def cache_parts(n):
        c = n // 2
        cols = head_cols(c)
        groups = 4
        span = vt.shape[2] // groups

        def keys(j):
            k = j % 2
            if j < 2:
                return jnp.concatenate([root[k, b, 0, :, cols] for b in range(n_root)], axis=0)
            key = jnp.concatenate([branch[k, b, 0, :, cols] for b in range(n_branch)], axis=0)
            mark = jnp.concatenate([kaug[k * n_branch + b] for b in range(n_branch)], axis=0)
            return jnp.concatenate([key, mark], axis=1)

        def queries(qbuf, y):
            query = jnp.concatenate([qbuf[n, z] for z in range(depth)], axis=0)
            first = lax.rem(n, 2) * depth
            mark = jnp.concatenate([qaug[y, first + z] for z in range(depth)], axis=0)
            return query, jnp.concatenate([query, mark], axis=1)

        def score(j, query):
            return matmul(keys(j), query[j // 2], ((1,), (1,)))

        query = queries(qfar, 1 - yy)
        scores = [score(j, query) for j in range(groups)]
        query = queries(qown, yy)
        for i in range(2):
            top = functools.reduce(
                jnp.maximum, [jnp.max(s, axis=0, keepdims=True) for s in scores]
            ) * UNIT
            later, out = [], None
            for j in range(groups):
                if i == 0:
                    later.append(score(j, query))
                w = jnp.exp2(scores[j] * UNIT - top).astype(jnp.bfloat16)
                part = matmul(vt[c, :, j * span : (j + 1) * span], w, ((1,), (0,)))
                out = part if out is None else out + part
            scores = later
            stat = jnp.concatenate([top, out[HD : HD + 1]], axis=0)
            if i == 0:
                put_o[n] = out[:HD].astype(jnp.bfloat16)
                put_s[n] = stat
                for copy in send_y(n):
                    copy.start()
            else:
                own_o[n] = out[:HD]
                own_s[n] = stat

    def merge(n):
        stat_a, stat_b = own_s[n], got_s[n]
        top = jnp.maximum(stat_a[0:1], stat_b[0:1])
        wa = jnp.exp2(stat_a[0:1] - top)
        wb = jnp.exp2(stat_b[0:1] - top)
        stat = jnp.concatenate([top, stat_a[1:2] * wa + stat_b[1:2] * wb], axis=0)
        out = own_o[n] * wa + got_o[n].astype(jnp.float32) * wb
        for z in range(depth):
            part = slice(z * rows, (z + 1) * rows)
            fold_o[n, z] = fold(out, part).astype(jnp.bfloat16)
            fold_s[n, z] = jnp.concatenate([stat[:, part]] * 2, axis=1)

    def finish(h):
        stats = [all_s[h, z] for z in range(depth)]
        own = tst[h]
        top = functools.reduce(jnp.maximum, [s[0:1] for s in stats] + [own[0:1]])
        scale = jnp.exp2(own[0:1] - top)
        number = tacc[h] * scale
        total = own[1:2] * scale
        for z in range(depth):
            factor = jnp.exp2(stats[z][0:1] - top)
            number = number + all_o[h, z].astype(jnp.float32) * factor
            total = total + stats[z][1:2] * factor
        out = number / total
        out = jnp.concatenate([out[:, :rows], out[:, rows:]], axis=0).T
        for s in range(steps):
            for g in range(GROUP):
                first = (s * GROUP + g) * req_here
                cols = pl.ds(pl.multiple_of((h * GROUP + g) * HD, HD), HD)
                out_ref[s, :, cols] = out[first : first + req_here].astype(jnp.bfloat16)

    for load in table_loads:
        load.wait()
    tables()
    gather_z_sent(0)
    gather_z_start(1)
    loads[2].wait()

    @pl.loop(0, chunks + LAG_LAST)
    def _(t):
        @pl.when(t < chunks)
        def _():
            gather_z_wait(t)
            gather_y(t).start()

        @pl.when(t < KVH // PAIR)
        def _():
            tail_part(t)

        @pl.when((lax.rem(t, 2) == 1) & (t < 2 * (HEADS - 2)))
        def _():
            gather_z_sent(t // 2 + 1)
            gather_z_start(t // 2 + 2)

        @pl.when(t == LAG_WORK - 1)
        def _():
            for load in loads[:2]:
                load.wait()
            for share in shares_in:
                share.wait_recv()

        @pl.when((t >= LAG_WORK - 1) & (t < HEADS + LAG_WORK - 1))
        def _():
            turn_values(t - LAG_WORK + 1)

        @pl.when((t >= LAG_WORK) & (t < chunks + LAG_WORK))
        def _():
            n = t - LAG_WORK
            gather_y(n).wait_recv()
            cache_parts(n)

        @pl.when((t >= LAG_MERGE) & (t < chunks + LAG_MERGE))
        def _():
            n = t - LAG_MERGE
            for copy in send_y(n):
                copy.wait_recv()
            merge(n)
            for o in range(1, depth):
                for copy in send_z(n, lax.rem(zz + o, depth)):
                    copy.start()

            @pl.when(lax.rem(n, 2) != core)
            def _():
                for copy in send_z(n, zz):
                    copy.start()

            @pl.when(lax.rem(n, 2) == core)
            def _():
                all_o[core * HEADS + n // 2, zz] = fold_o[n, zz]
                all_s[core * HEADS + n // 2, zz] = fold_s[n, zz]

        for c in range(HEADS):

            @pl.when(t == 2 * c + core + LAG_LAST)
            def _(c=c):
                for k, count in ((core, depth - 1), (1 - core, depth)):
                    h = k * HEADS + c
                    for copy in send_z_in(h, count):
                        copy.wait_recv()
                    finish(h)

    gather_z_sent(HEADS - 1)

    @pl.loop(0, chunks)
    def _(n):
        gather_y(n).wait_send()
        for copy in send_y(n):
            copy.wait_send()

        @pl.when(lax.rem(n, 2) == core)
        def _():
            for copy in send_z_sent(n, depth - 1):
                copy.wait_send()

        @pl.when(lax.rem(n, 2) != core)
        def _():
            for copy in send_z_sent(n, depth):
                copy.wait_send()

    for share in shares:
        share.wait_send()


def body(queries, new_kv, root_kv, branch_kv, tail_kv, parent, node_len, leaf_of, branch_slot):
    devices = lax.axis_size("kv")
    steps, req_here, _ = queries.shape
    rows = steps * req_here * GROUP
    depth = devices // 4
    chunks = 2 * HEADS
    lanes = depth * rows
    n_root, _, block_len, _ = root_kv.shape
    n_branch = branch_kv.shape[0]
    tokens = 2 * (n_root + n_branch) * block_len
    bf, f32 = jnp.bfloat16, jnp.float32
    vmem = pl.BlockSpec(memory_space=pltpu.VMEM)
    hbm = pl.BlockSpec(memory_space=pl.ANY)
    dma = pltpu.SemaphoreType.DMA
    return pl.pallas_call(
        functools.partial(kernel, devices, steps, req_here),
        out_shape=jax.ShapeDtypeStruct(queries.shape, bf),
        in_specs=[hbm] * 9,
        out_specs=vmem,
        scratch_shapes=[
            pltpu.SMEM(parent.shape, jnp.int32),
            pltpu.SMEM(node_len.shape, jnp.int32),
            pltpu.SMEM(leaf_of.shape, jnp.int32),
            pltpu.SMEM(branch_slot.shape, jnp.int32),
            pltpu.VMEM(queries.shape, bf),
            pltpu.VMEM(new_kv.shape, bf),
            pltpu.VMEM((KVH, rows, HD), bf),
            pltpu.VMEM((chunks, depth, rows, HD), bf),
            pltpu.VMEM((chunks, depth, rows, HD), bf),
            pltpu.VMEM((2, n_root, 2, block_len, HEADS * HD), bf),
            pltpu.VMEM((2, n_branch, 2, block_len, HEADS * HD), bf),
            pltpu.VMEM(tail_kv.shape, bf),
            pltpu.VMEM((HEADS, HD + EXTRA, tokens), bf),
            pltpu.VMEM((2 * n_branch, block_len, HD), bf),
            pltpu.VMEM((2, depth * 2, rows, HD), bf),
            pltpu.VMEM((req_here, PAIR * rows), jnp.int32),
            pltpu.VMEM((2, 16, KVH * HD), bf),
            pltpu.VMEM((chunks, HD, lanes), f32),
            pltpu.VMEM((chunks, 2, lanes), f32),
            pltpu.VMEM((chunks, HD, lanes), bf),
            pltpu.VMEM((chunks, 2, lanes), f32),
            pltpu.VMEM((chunks, HD, lanes), bf),
            pltpu.VMEM((chunks, 2, lanes), f32),
            pltpu.VMEM((chunks, depth, HD // 2, 2 * rows), bf),
            pltpu.VMEM((chunks, depth, 2, 2 * rows), f32),
            pltpu.VMEM((KVH, depth, HD // 2, 2 * rows), bf),
            pltpu.VMEM((KVH, depth, 2, 2 * rows), f32),
            pltpu.VMEM((KVH, HD // 2, 2 * rows), f32),
            pltpu.VMEM((KVH, 2, 2 * rows), f32),
            dma((9,)), dma((2,)), dma((2,)),
            dma((HEADS, 2)), dma((chunks,)), dma((chunks,)), dma((chunks,)),
            dma((chunks, 2)), dma((chunks, 2)), dma((chunks, 2)), dma((KVH, 2)),
        ],
        compiler_params=pltpu.CompilerParams(
            collective_id=0, has_side_effects=True, vmem_limit_bytes=56 * 1024 * 1024
        ),
    )(parent, node_len, leaf_of, branch_slot, queries, new_kv, root_kv, branch_kv, tail_kv)


def solution(mesh):
    return jax.shard_map(
        body,
        mesh=mesh,
        in_specs=(
            P(None, ("groups", "kv"), None),
            P(None, None, ("groups", "kv"), None),
            P(("groups", "kv"), None, None, None),
            P(("groups", "kv"), None, None, None),
            P(("groups", "kv"), None, None, None),
            P("groups"),
            P("groups"),
            P("groups"),
            P("groups"),
        ),
        out_specs=P(None, ("groups", "kv"), None),
        check_vma=False,
    )
```

```python
import functools

import jax
import jax.numpy as jnp
from jax import lax
from jax.experimental import pallas as pl
from jax.experimental.pallas import tpu as pltpu
from jax.sharding import PartitionSpec as P

QH = 128
KVH = 8
HD = 128
GROUP = QH // KVH
HEADS = KVH // 2
PAIR = 2
MASKED = -1e30
UNIT = HD**-0.5 * 1.4426950408889634
EXTRA = 16
LAG_WORK = 3
LAG_MERGE = 5
LAG_LAST = 7


def matmul(a, b, dims):
    return lax.dot_general(a, b, (dims, ((), ())), preferred_element_type=jnp.float32)


def attend(scores):
    top = functools.reduce(jnp.maximum, [jnp.max(s, axis=0, keepdims=True) for s in scores]) * UNIT
    weights = [jnp.exp2(s * UNIT - top) for s in scores]
    return top, weights


def kernel(
    devices, steps, req_here,
    parent_hbm, node_len_hbm, leaf_hbm, slot_hbm,
    q_hbm, new_hbm, root_hbm, branch_hbm, tail_hbm,
    out_ref,
    parent, node_len, leaf_of, branch_slot, q_in, new_ref, qsrc, qown, qfar, root, branch, tail, vt, kaug, qaug, tl_ref, fresh,
    own_o, own_s, put_o, put_s, got_o, got_s, fold_o, fold_s, all_o, all_s, tacc, tst,
    hbm_sem, kv_s, kv_r, gz_s, gz_r, gy_s, gy_r, y_s, y_r, z_s, z_r,
):
    depth = devices // 4
    rows = steps * req_here * GROUP
    chunks = 2 * HEADS
    lanes = depth * rows
    half_dim = HD // 2
    me = lax.axis_index("kv")
    core = lax.rem(me, 2)
    yy = lax.rem(me // 2, 2)
    zz = me // 4
    core_peer = me + 1 - 2 * core
    y_peer = me + 2 - 4 * yy
    n_root = root.shape[1]
    n_branch = branch.shape[1]
    block_len = root.shape[3]
    blocks = 2 * (n_root + n_branch)
    half_cols = HEADS * HD

    def device(z, k):
        return z * 4 + yy * 2 + k

    def remote(src, dst, send, recv, peer):
        return pltpu.make_async_remote_copy(
            src_ref=src, dst_ref=dst, send_sem=send, recv_sem=recv,
            device_id={"kv": peer}, device_id_type=pl.DeviceIdType.MESH,
        )

    def half(ref, k):
        return ref.at[:, :, :, pl.ds(pl.multiple_of(k * half_cols, half_cols), half_cols)]

    first_loads = [
        pltpu.make_async_copy(q_hbm, q_in, hbm_sem.at[3]),
        pltpu.make_async_copy(new_hbm, new_ref, hbm_sem.at[4]),
    ]
    table_loads = [
        pltpu.make_async_copy(parent_hbm, parent, hbm_sem.at[5]),
        pltpu.make_async_copy(node_len_hbm, node_len, hbm_sem.at[6]),
        pltpu.make_async_copy(leaf_hbm, leaf_of, hbm_sem.at[7]),
        pltpu.make_async_copy(slot_hbm, branch_slot, hbm_sem.at[8]),
    ]
    loads = [
        pltpu.make_async_copy(half(root_hbm, core), root.at[core], hbm_sem.at[0]),
        pltpu.make_async_copy(half(branch_hbm, core), branch.at[core], hbm_sem.at[1]),
        pltpu.make_async_copy(tail_hbm, tail, hbm_sem.at[2]),
    ]
    shares = [
        remote(half(root_hbm, 1 - core), root.at[core], kv_s.at[0], kv_r.at[0], core_peer),
        remote(half(branch_hbm, 1 - core), branch.at[core], kv_s.at[1], kv_r.at[1], core_peer),
    ]
    shares_in = [
        remote(root.at[core], root.at[1 - core], kv_s.at[0], kv_r.at[0], core_peer),
        remote(branch.at[core], branch.at[1 - core], kv_s.at[1], kv_r.at[1], core_peer),
    ]
    for load in first_loads + table_loads + loads:
        load.start()

    barrier = pltpu.get_barrier_semaphore()
    peers = [core_peer, y_peer]
    for o in range(1, depth):
        z = lax.rem(zz + o, depth)
        peers += [device(z, core), device(z, 1 - core)]
    for peer in peers:
        pl.semaphore_signal(
            barrier, inc=1, device_id={"kv": peer}, device_id_type=pl.DeviceIdType.MESH
        )

    def lay_out(h):
        pieces = []
        for s in range(steps):
            for g in range(GROUP):
                cols = pl.ds(pl.multiple_of((h * GROUP + g) * HD, HD), HD)
                pieces.append(q_in[s, :, cols].astype(jnp.float32))
        qsrc[h] = jnp.concatenate(pieces, axis=0).astype(jnp.bfloat16)

    for load in first_loads:
        load.wait()

    lay_out(0)
    lay_out(HEADS)

    pl.semaphore_wait(barrier, len(peers))

    def gather_z_start(c):
        dst = qown.at[c * 2 + core, zz]
        for k in (core, 1 - core):
            for o in range(depth - 1, 0, -1):
                z = lax.rem(zz + o, depth)
                gather_z(c, k, dst, device(z, k)).start()
        gather_z(c, 1 - core, dst, core_peer).start()
        qown[c * 2 + core, zz] = qsrc[core * HEADS + c]

    def gather_z(c, k, dst, peer):
        return remote(
            qsrc.at[k * HEADS + c], dst, gz_s.at[c, lax.rem(k + core, 2)],
            gz_r.at[c * 2 + core], peer,
        )

    gather_z_start(0)
    for share in shares:
        share.start()

    @pl.loop(1, HEADS)
    def _(c):
        lay_out(c)
        lay_out(HEADS + c)

    def gather_z_wait(n):
        def wait(count):
            part = qown.at[n, pl.ds(0, count)]
            remote(part, part, gz_s.at[0, 0], gz_r.at[n], y_peer).wait_recv()

        @pl.when(lax.rem(n, 2) == core)
        def _():
            wait(depth - 1)

        @pl.when(lax.rem(n, 2) != core)
        def _():
            wait(depth)

    def gather_z_sent(c):
        for other in range(2):
            part = qown.at[0, pl.ds(0, depth - 1 + other)]
            remote(part, part, gz_s.at[c, other], gz_r.at[0], y_peer).wait_send()

    def gather_y(n):
        return remote(qown.at[n], qfar.at[n], gy_s.at[n], gy_r.at[n], y_peer)

    def send_y(n):
        return (
            remote(put_o.at[n], got_o.at[n], y_s.at[n, 0], y_r.at[n, 0], y_peer),
            remote(put_s.at[n], got_s.at[n], y_s.at[n, 1], y_r.at[n, 1], y_peer),
        )

    def send_z(n, z):
        c = n // 2
        h = core * HEADS + c
        peer = device(z, lax.rem(n, 2))
        return (
            remote(fold_o.at[n, z], all_o.at[h, zz], z_s.at[n, 0], z_r.at[h, 0], peer),
            remote(fold_s.at[n, z], all_s.at[h, zz], z_s.at[n, 1], z_r.at[h, 1], peer),
        )

    def send_z_in(h, count):
        part = pl.ds(0, count)
        return (
            remote(all_o.at[h, part], all_o.at[h, part], z_s.at[0, 0], z_r.at[h, 0], y_peer),
            remote(all_s.at[h, part], all_s.at[h, part], z_s.at[0, 1], z_r.at[h, 1], y_peer),
        )

    def send_z_sent(n, count):
        part = pl.ds(0, count)
        return (
            remote(fold_o.at[n, part], fold_o.at[n, part], z_s.at[n, 0], z_r.at[0, 0], y_peer),
            remote(fold_s.at[n, part], fold_s.at[n, part], z_s.at[n, 1], z_r.at[0, 1], y_peer),
        )

    def tables():
        slots = 2 * n_branch
        first_slot = (me // 2) * slots
        slot_nodes = [branch_slot[first_slot + j] for j in range(slots)]

        def count_rank(i, ranks):
            node = branch_slot[i]
            return tuple(
                rank + jnp.where((node == slot_nodes[j]) & (i < first_slot + j), 1, 0)
                for j, rank in enumerate(ranks)
            )

        ranks = lax.fori_loop(0, branch_slot.shape[0], count_rank, (jnp.int32(0),) * slots)
        token = lax.broadcasted_iota(jnp.int32, (block_len, HD), 0)
        lane = lax.broadcasted_iota(jnp.int32, (block_len, HD), 1)
        for j in range(slots):
            owned = node_len[jnp.minimum(slot_nodes[j], node_len.shape[0] - 1)]
            fill = jnp.clip(owned - ranks[j] * block_len, 0, block_len)
            fill = jnp.where(slot_nodes[j] < node_len.shape[0], fill, 0)
            x = jnp.where(lane == j, 1.0, 0.0)
            x = jnp.where((lane == slots) & (token >= fill), MASKED, x)
            kaug[j] = x.astype(jnp.bfloat16)
        tile = 16
        lane = lax.broadcasted_iota(jnp.int32, (tile, HD), 1)
        which = lax.rem(lax.broadcasted_iota(jnp.int32, (tile, HD), 0), req_here)
        slot_of_lane = jnp.full((tile, HD), -1, jnp.int32)
        for j in range(slots):
            slot_of_lane = jnp.where(lane == j, slot_nodes[j], slot_of_lane)
        for y in range(2):
            for i in range(2 * depth):
                owner = (i % depth) * 4 + y * 2 + i // depth
                node = jnp.zeros((tile, HD), jnp.int32)
                for r in range(req_here):
                    node = jnp.where(which == r, parent[leaf_of[owner * req_here + r]], node)
                x = jnp.where(node == slot_of_lane, 0.0, MASKED)
                x = jnp.where(lane < slots, x, jnp.where(lane == slots, 1.0, 0.0))
                qaug[y, i] = jnp.concatenate([x] * (rows // tile), axis=0).astype(jnp.bfloat16)
        lane = lax.broadcasted_iota(jnp.int32, (1, PAIR * rows), 1)
        for r in range(req_here):
            tl_ref[r : r + 1, :] = jnp.where(
                lax.rem(lane, req_here) == r, node_len[leaf_of[me * req_here + r]], 0
            )
        fresh[...] = jnp.zeros_like(fresh)
        for s in range(steps):
            for kv in range(2):
                fresh[kv, s * req_here : (s + 1) * req_here, :] = new_ref[s, kv]
        vt[:, HD:, :] = jnp.ones((HEADS, EXTRA, vt.shape[2]), jnp.bfloat16)

    def head_cols(k):
        return pl.ds(pl.multiple_of(k * HD, HD), HD)

    def fold(x, part):
        return jnp.concatenate([x[:half_dim, part], x[half_dim:, part]], axis=1)

    def tail_part(p):
        query = [qsrc[p * PAIR + h] for h in range(PAIR)]
        cols = [head_cols(p * PAIR + h) for h in range(PAIR)]
        scores = []
        for r in range(req_here):
            s = jnp.concatenate(
                [matmul(tail[r, 0, :, cols[h]], query[h], ((1,), (1,))) for h in range(PAIR)], axis=1
            )
            token = lax.broadcasted_iota(jnp.int32, s.shape, 0)
            scores.append(jnp.where(token < tl_ref[r : r + 1, :], s, MASKED))
        s = jnp.concatenate(
            [matmul(fresh[0, :, cols[h]], query[h], ((1,), (1,))) for h in range(PAIR)], axis=1
        )
        token = lax.broadcasted_iota(jnp.int32, s.shape, 0)
        lane = lax.broadcasted_iota(jnp.int32, s.shape, 1)
        lane_step = lax.rem(lane // (GROUP * req_here), steps)
        live = (token < steps * req_here) & (lax.rem(token, req_here) == lax.rem(lane, req_here))
        live = live & (token // req_here <= lane_step)
        scores.append(jnp.where(live, s, MASKED))
        top, weights = attend(scores)
        total = functools.reduce(jnp.add, [jnp.sum(w, axis=0, keepdims=True) for w in weights])
        weights = [w.astype(jnp.bfloat16) for w in weights]
        stat = jnp.concatenate([top, total], axis=0)
        for h in range(PAIR):
            values = [tail[r, 1, :, cols[h]] for r in range(req_here)] + [fresh[1, :, cols[h]]]
            part = slice(h * rows, (h + 1) * rows)
            out = functools.reduce(
                jnp.add, [matmul(v, w[:, part], ((0,), (0,))) for v, w in zip(values, weights)]
            )
            tacc[p * PAIR + h] = jnp.concatenate([out[:half_dim], out[half_dim:]], axis=1)
            tst[p * PAIR + h] = jnp.concatenate([stat[:, part]] * 2, axis=1)

    def turn_values(c):
        cols = head_cols(c)
        for k in range(2):
            for b in range(n_root):
                i = k * n_root + b
                vt[c, :HD, i * block_len : (i + 1) * block_len] = root[k, b, 1, :, cols].T
            for b in range(n_branch):
                i = 2 * n_root + k * n_branch + b
                vt[c, :HD, i * block_len : (i + 1) * block_len] = branch[k, b, 1, :, cols].T

    def cache_parts(n):
        c = n // 2
        cols = head_cols(c)
        groups = 4
        span = vt.shape[2] // groups

        def keys(j):
            k = j % 2
            if j < 2:
                return jnp.concatenate([root[k, b, 0, :, cols] for b in range(n_root)], axis=0)
            key = jnp.concatenate([branch[k, b, 0, :, cols] for b in range(n_branch)], axis=0)
            mark = jnp.concatenate([kaug[k * n_branch + b] for b in range(n_branch)], axis=0)
            return jnp.concatenate([key, mark], axis=1)

        def queries(qbuf, y):
            query = jnp.concatenate([qbuf[n, z] for z in range(depth)], axis=0)
            first = lax.rem(n, 2) * depth
            mark = jnp.concatenate([qaug[y, first + z] for z in range(depth)], axis=0)
            return query, jnp.concatenate([query, mark], axis=1)

        def score(j, query):
            return matmul(keys(j), query[j // 2], ((1,), (1,)))

        query = queries(qfar, 1 - yy)
        scores = [score(j, query) for j in range(groups)]
        query = queries(qown, yy)
        for i in range(2):
            top = functools.reduce(
                jnp.maximum, [jnp.max(s, axis=0, keepdims=True) for s in scores]
            ) * UNIT
            later, out = [], None
            for j in range(groups):
                if i == 0:
                    later.append(score(j, query))
                w = jnp.exp2(scores[j] * UNIT - top).astype(jnp.bfloat16)
                part = matmul(vt[c, :, j * span : (j + 1) * span], w, ((1,), (0,)))
                out = part if out is None else out + part
            scores = later
            stat = jnp.concatenate([top, out[HD : HD + 1]], axis=0)
            if i == 0:
                put_o[n] = out[:HD].astype(jnp.bfloat16)
                put_s[n] = stat
                for copy in send_y(n):
                    copy.start()
            else:
                own_o[n] = out[:HD]
                own_s[n] = stat

    def merge(n):
        stat_a, stat_b = own_s[n], got_s[n]
        top = jnp.maximum(stat_a[0:1], stat_b[0:1])
        wa = jnp.exp2(stat_a[0:1] - top)
        wb = jnp.exp2(stat_b[0:1] - top)
        stat = jnp.concatenate([top, stat_a[1:2] * wa + stat_b[1:2] * wb], axis=0)
        out = own_o[n] * wa + got_o[n].astype(jnp.float32) * wb
        for z in range(depth):
            part = slice(z * rows, (z + 1) * rows)
            fold_o[n, z] = fold(out, part).astype(jnp.bfloat16)
            fold_s[n, z] = jnp.concatenate([stat[:, part]] * 2, axis=1)

    def finish(h):
        stats = [all_s[h, z] for z in range(depth)]
        own = tst[h]
        top = functools.reduce(jnp.maximum, [s[0:1] for s in stats] + [own[0:1]])
        scale = jnp.exp2(own[0:1] - top)
        number = tacc[h] * scale
        total = own[1:2] * scale
        for z in range(depth):
            factor = jnp.exp2(stats[z][0:1] - top)
            number = number + all_o[h, z].astype(jnp.float32) * factor
            total = total + stats[z][1:2] * factor
        out = number / total
        out = jnp.concatenate([out[:, :rows], out[:, rows:]], axis=0).T
        for s in range(steps):
            for g in range(GROUP):
                first = (s * GROUP + g) * req_here
                cols = pl.ds(pl.multiple_of((h * GROUP + g) * HD, HD), HD)
                out_ref[s, :, cols] = out[first : first + req_here].astype(jnp.bfloat16)

    for load in table_loads:
        load.wait()
    tables()
    gather_z_sent(0)
    gather_z_start(1)
    loads[2].wait()

    @pl.loop(0, chunks + LAG_LAST)
    def _(t):
        @pl.when(t < chunks)
        def _():
            gather_z_wait(t)
            gather_y(t).start()

        @pl.when(t < KVH // PAIR)
        def _():
            tail_part(t)

        @pl.when((lax.rem(t, 2) == 1) & (t < 2 * (HEADS - 2)))
        def _():
            gather_z_sent(t // 2 + 1)
            gather_z_start(t // 2 + 2)

        @pl.when(t == LAG_WORK - 1)
        def _():
            for load in loads[:2]:
                load.wait()
            for share in shares_in:
                share.wait_recv()

        @pl.when((t >= LAG_WORK - 1) & (t < HEADS + LAG_WORK - 1))
        def _():
            turn_values(t - LAG_WORK + 1)

        @pl.when((t >= LAG_WORK) & (t < chunks + LAG_WORK))
        def _():
            n = t - LAG_WORK
            gather_y(n).wait_recv()
            cache_parts(n)

        @pl.when((t >= LAG_MERGE) & (t < chunks + LAG_MERGE))
        def _():
            n = t - LAG_MERGE
            for copy in send_y(n):
                copy.wait_recv()
            merge(n)
            for o in range(1, depth):
                for copy in send_z(n, lax.rem(zz + o, depth)):
                    copy.start()

            @pl.when(lax.rem(n, 2) != core)
            def _():
                for copy in send_z(n, zz):
                    copy.start()

            @pl.when(lax.rem(n, 2) == core)
            def _():
                all_o[core * HEADS + n // 2, zz] = fold_o[n, zz]
                all_s[core * HEADS + n // 2, zz] = fold_s[n, zz]

            gather_y(n).wait_send()
            for copy in send_y(n):
                copy.wait_send()

        for c in range(HEADS):

            @pl.when(t == 2 * c + core + LAG_LAST)
            def _(c=c):
                for k, count in ((core, depth - 1), (1 - core, depth)):
                    h = k * HEADS + c
                    for copy in send_z_in(h, count):
                        copy.wait_recv()
                    finish(h)

    gather_z_sent(HEADS - 1)

    @pl.loop(0, chunks)
    def _(n):
        @pl.when(lax.rem(n, 2) == core)
        def _():
            for copy in send_z_sent(n, depth - 1):
                copy.wait_send()

        @pl.when(lax.rem(n, 2) != core)
        def _():
            for copy in send_z_sent(n, depth):
                copy.wait_send()

    for share in shares:
        share.wait_send()


def body(queries, new_kv, root_kv, branch_kv, tail_kv, parent, node_len, leaf_of, branch_slot):
    devices = lax.axis_size("kv")
    steps, req_here, _ = queries.shape
    rows = steps * req_here * GROUP
    depth = devices // 4
    chunks = 2 * HEADS
    lanes = depth * rows
    n_root, _, block_len, _ = root_kv.shape
    n_branch = branch_kv.shape[0]
    tokens = 2 * (n_root + n_branch) * block_len
    bf, f32 = jnp.bfloat16, jnp.float32
    vmem = pl.BlockSpec(memory_space=pltpu.VMEM)
    hbm = pl.BlockSpec(memory_space=pl.ANY)
    dma = pltpu.SemaphoreType.DMA
    return pl.pallas_call(
        functools.partial(kernel, devices, steps, req_here),
        out_shape=jax.ShapeDtypeStruct(queries.shape, bf),
        in_specs=[hbm] * 9,
        out_specs=vmem,
        scratch_shapes=[
            pltpu.SMEM(parent.shape, jnp.int32),
            pltpu.SMEM(node_len.shape, jnp.int32),
            pltpu.SMEM(leaf_of.shape, jnp.int32),
            pltpu.SMEM(branch_slot.shape, jnp.int32),
            pltpu.VMEM(queries.shape, bf),
            pltpu.VMEM(new_kv.shape, bf),
            pltpu.VMEM((KVH, rows, HD), bf),
            pltpu.VMEM((chunks, depth, rows, HD), bf),
            pltpu.VMEM((chunks, depth, rows, HD), bf),
            pltpu.VMEM((2, n_root, 2, block_len, HEADS * HD), bf),
            pltpu.VMEM((2, n_branch, 2, block_len, HEADS * HD), bf),
            pltpu.VMEM(tail_kv.shape, bf),
            pltpu.VMEM((HEADS, HD + EXTRA, tokens), bf),
            pltpu.VMEM((2 * n_branch, block_len, HD), bf),
            pltpu.VMEM((2, depth * 2, rows, HD), bf),
            pltpu.VMEM((req_here, PAIR * rows), jnp.int32),
            pltpu.VMEM((2, 16, KVH * HD), bf),
            pltpu.VMEM((chunks, HD, lanes), f32),
            pltpu.VMEM((chunks, 2, lanes), f32),
            pltpu.VMEM((chunks, HD, lanes), bf),
            pltpu.VMEM((chunks, 2, lanes), f32),
            pltpu.VMEM((chunks, HD, lanes), bf),
            pltpu.VMEM((chunks, 2, lanes), f32),
            pltpu.VMEM((chunks, depth, HD // 2, 2 * rows), bf),
            pltpu.VMEM((chunks, depth, 2, 2 * rows), f32),
            pltpu.VMEM((KVH, depth, HD // 2, 2 * rows), bf),
            pltpu.VMEM((KVH, depth, 2, 2 * rows), f32),
            pltpu.VMEM((KVH, HD // 2, 2 * rows), f32),
            pltpu.VMEM((KVH, 2, 2 * rows), f32),
            dma((9,)), dma((2,)), dma((2,)),
            dma((HEADS, 2)), dma((chunks,)), dma((chunks,)), dma((chunks,)),
            dma((chunks, 2)), dma((chunks, 2)), dma((chunks, 2)), dma((KVH, 2)),
        ],
        compiler_params=pltpu.CompilerParams(
            collective_id=0, has_side_effects=True, vmem_limit_bytes=56 * 1024 * 1024
        ),
    )(parent, node_len, leaf_of, branch_slot, queries, new_kv, root_kv, branch_kv, tail_kv)


def solution(mesh):
    return jax.shard_map(
        body,
        mesh=mesh,
        in_specs=(
            P(None, ("groups", "kv"), None),
            P(None, None, ("groups", "kv"), None),
            P(("groups", "kv"), None, None, None),
            P(("groups", "kv"), None, None, None),
            P(("groups", "kv"), None, None, None),
            P("groups"),
            P("groups"),
            P("groups"),
            P("groups"),
        ),
        out_specs=P(None, ("groups", "kv"), None),
        check_vma=False,
    )
```
